32 devices in a mesh: dp: 8 (over y, x, core), tensor: 4 (over z).
Axes of the slice: x: 2, y: 2, z: 4, core: 2. Of those that a mesh axis runs over, the one named last changes fastest.
Arguments:
- block_in: float32 [8, 256, 1024], P('dp', None, 'tensor'), may hold values from -40 to 40
- norm_in: float32 [1024], replicated, may hold values from 0.5 to 1.5
- w_in: bfloat16 [1024, 3, 1024], P(None, None, 'tensor'), may hold values from -0.1875 to 0.1875
- conv_w: float32 [3, 1024], P(None, 'tensor'), may hold values from -3 to 3
- w_out: bfloat16 [1024, 1024], P('tensor'), may hold values from -0.1875 to 0.1875
- norm_mid: float32 [1024], replicated, may hold values from 0.5 to 1.5
- w_gate: bfloat16 [1024, 4608], P(None, 'tensor'), may hold values from -0.1875 to 0.1875
- w_up: bfloat16 [1024, 4608], P(None, 'tensor'), may hold values from -0.1875 to 0.1875
- w_down: bfloat16 [4608, 1024], P('tensor'), may hold values from -0.09375 to 0.09375
- cot: float32 [8, 256, 1024], P('dp', None, 'tensor'), may hold values from -6 to 6
Outputs:
- block_out: float32 [8, 256, 1024], P('dp', None, 'tensor')
- grad_in: float32 [8, 256, 1024], P('dp', None, 'tensor')
- grad_norm_in: float32 [1024], P('tensor')
- grad_w_in: float32 [1024, 3, 1024], P('dp', None, 'tensor')
- grad_conv: float32 [3, 1024], P(None, 'tensor')
- grad_w_out: float32 [1024, 1024], P('tensor', 'dp')
- grad_norm_mid: float32 [1024], P('tensor')
- grad_w_gate: float32 [1024, 4608], P('dp', 'tensor')
- grad_w_up: float32 [1024, 4608], P('dp', 'tensor')
- grad_w_down: float32 [4608, 1024], P('tensor', 'dp')
The draws below stay inside these ranges and needn't reach their ends.
All inputs are finite; a program needn't handle non-finite values.
Results may differ from the reference program's by a relative error of at most 0.0079.
Values may be sent and summed in bfloat16 or wider, within the bound.
No kernel may reach another device: no remote copies, remote signals or barrier semaphores. Data moves between devices by JAX's collectives and lax.ppermute only.
A program may use at most 128 MiB of HBM per device.

```python
import jax
import jax.numpy as jnp
from jax import lax

D = 1024
FF = 4608
KW = 3
LEN = 256
SEQS = 8


def draw_block_in(key, part):
    key_one = jax.random.fold_in(key, 11)
    key_two = jax.random.fold_in(key, 12)
    place = jnp.arange(D, dtype=jnp.float32) / (D - 1.0)
    rough = jnp.exp(jax.random.uniform(key_two, (D,), jnp.float32, -0.3, 0.3))
    scales = 0.5 * jnp.exp(place * jnp.log(8.0)) * rough
    base = jnp.clip(jax.random.normal(key_one, (SEQS, LEN, D), jnp.float32), -6.0, 6.0)
    return (base * scales).astype(jnp.float32)


def block_levels(key, shape, pieces, low, high):
    def one(axis_at, parts):
        heights = jax.random.uniform(jax.random.fold_in(jax.random.fold_in(key, 6), axis_at), (parts,), jnp.float32, low / len(pieces), high / len(pieces))
        return jnp.repeat(jnp.exp(heights), shape[axis_at] // parts).reshape((-1,) + (1,) * (len(shape) - axis_at - 1))

    gain = one(*pieces[0])
    for cut in pieces[1:]:
        gain = gain * one(*cut)
    return gain


def normal_values(own_key, shape, width, limit, split=(), kind=jnp.bfloat16):
    values = width * jax.random.normal(own_key, shape, jnp.float32)
    if split:
        values = values * block_levels(own_key, shape, split, -0.22, 0.18)
    return jnp.clip(values, -limit, limit).astype(kind)


def setup_inputs(seed: int = 0) -> dict:
    seeds = jax.random.split(jax.random.key(seed), 11)
    return {
        "block_in": draw_block_in(jax.random.fold_in(seeds[10], 71), 0),
        "norm_in": jnp.clip(1.0 + 0.1 * jax.random.normal(seeds[1], (D,), jnp.float32), 0.5, 1.5),
        "w_in": normal_values(seeds[2], (D, 3, D), D ** -0.5, 0.1875, ((2, 4),)),
        "conv_w": normal_values(seeds[3], (KW, D), 0.6, 3.0, ((1, 4),), jnp.float32),
        "w_out": normal_values(seeds[4], (D, D), D ** -0.5, 0.1875, ((0, 4),)),
        "norm_mid": jnp.clip(1.0 + 0.1 * jax.random.normal(seeds[5], (D,), jnp.float32), 0.5, 1.5),
        "w_gate": normal_values(seeds[6], (D, FF), D ** -0.5, 0.1875, ((1, 4),)),
        "w_up": normal_values(seeds[7], (D, FF), D ** -0.5, 0.1875, ((1, 4),)),
        "w_down": normal_values(seeds[8], (FF, D), FF ** -0.5, 0.09375, ((0, 4),)),
        "cot": normal_values(seeds[9], (SEQS, LEN, D), 1.0, 6.0, ((0, 8), (2, 4)), jnp.float32),
    }


EPS = 1e-05

def back_shift(arr, k):
    return jnp.concatenate([jnp.zeros((k, arr.shape[1]), jnp.float32), arr[:-k]], axis=0)

def fore_shift(arr, k):
    return jnp.concatenate([arr[k:], jnp.zeros((k, arr.shape[1]), jnp.float32)], axis=0)

def one_sequence(xin, gy, norm_in, w_flat, conv_w, w_out, norm_mid, w_gate, w_up, w_down):
    q1 = lax.rsqrt(lax.optimization_barrier(jnp.mean(xin * xin, axis=1, keepdims=True)) + EPS)
    n1 = xin * q1
    h1 = (n1 * norm_in).astype(jnp.bfloat16)
    proj = jnp.dot(h1, w_flat, preferred_element_type=jnp.float32)
    bgate = proj[:, :D]
    cgate = proj[:, D:2 * D]
    xval = proj[:, 2 * D:]
    vmix = bgate * xval
    conv = conv_w[0] * vmix + conv_w[1] * back_shift(vmix, 1) + conv_w[2] * back_shift(vmix, 2)
    zmix = (cgate * conv).astype(jnp.bfloat16)
    resid = xin + jnp.dot(zmix, w_out, preferred_element_type=jnp.float32)
    q2 = lax.rsqrt(lax.optimization_barrier(jnp.mean(resid * resid, axis=1, keepdims=True)) + EPS)
    n2 = resid * q2
    h2 = (n2 * norm_mid).astype(jnp.bfloat16)
    gpre = jnp.dot(h2, w_gate, preferred_element_type=jnp.float32)
    upre = jnp.dot(h2, w_up, preferred_element_type=jnp.float32)
    sg = jax.nn.sigmoid(gpre)
    act = (gpre * sg * upre).astype(jnp.bfloat16)
    out = resid + jnp.dot(act, w_down, preferred_element_type=jnp.float32)
    cotb = gy.astype(jnp.bfloat16)
    g_down = jnp.dot(act.T, cotb, preferred_element_type=jnp.float32)
    dact = jnp.dot(cotb, w_down.T, preferred_element_type=jnp.float32)
    dgate = (dact * upre * sg * (1.0 + gpre * (1.0 - sg))).astype(jnp.bfloat16)
    dup = (dact * gpre * sg).astype(jnp.bfloat16)
    g_gate = jnp.dot(h2.T, dgate, preferred_element_type=jnp.float32)
    g_up = jnp.dot(h2.T, dup, preferred_element_type=jnp.float32)
    dh2 = jnp.dot(dgate, w_gate.T, preferred_element_type=jnp.float32) + jnp.dot(dup, w_up.T, preferred_element_type=jnp.float32)
    g_mid = lax.optimization_barrier(jnp.sum(dh2 * n2, axis=0))
    e2 = dh2 * norm_mid
    dres = gy + q2 * (e2 - n2 * lax.optimization_barrier(jnp.mean(e2 * n2, axis=1, keepdims=True)))
    dresb = dres.astype(jnp.bfloat16)
    g_out = jnp.dot(zmix.T, dresb, preferred_element_type=jnp.float32)
    dz = jnp.dot(dresb, w_out.T, preferred_element_type=jnp.float32)
    dcg = dz * conv
    dconv = dz * cgate
    g_conv = jnp.stack([lax.optimization_barrier(jnp.sum(dconv * vmix, axis=0)), lax.optimization_barrier(jnp.sum(dconv * back_shift(vmix, 1), axis=0)), lax.optimization_barrier(jnp.sum(dconv * back_shift(vmix, 2), axis=0))])
    dv = conv_w[0] * dconv + conv_w[1] * fore_shift(dconv, 1) + conv_w[2] * fore_shift(dconv, 2)
    dproj = jnp.concatenate([dv * xval, dcg, dv * bgate], axis=1).astype(jnp.bfloat16)
    g_in = jnp.dot(h1.T, dproj, preferred_element_type=jnp.float32)
    dh1 = jnp.dot(dproj, w_flat.T, preferred_element_type=jnp.float32)
    g_norm = lax.optimization_barrier(jnp.sum(dh1 * n1, axis=0))
    e1 = dh1 * norm_in
    dxin = dres + q1 * (e1 - n1 * lax.optimization_barrier(jnp.mean(e1 * n1, axis=1, keepdims=True)))
    return (out, dxin, (g_norm, g_in, g_conv, g_out, g_mid, g_gate, g_up, g_down))

def reference(block_in, norm_in, w_in, conv_w, w_out, norm_mid, w_gate, w_up, w_down, cot):
    w_flat = w_in.reshape(D, 3 * D)
    zeros = (jnp.zeros((D,), jnp.float32), jnp.zeros((D, 3 * D), jnp.float32), jnp.zeros((KW, D), jnp.float32), jnp.zeros((D, D), jnp.float32), jnp.zeros((D,), jnp.float32), jnp.zeros((D, FF), jnp.float32), jnp.zeros((D, FF), jnp.float32), jnp.zeros((FF, D), jnp.float32))

    def step(carry, pair):
        out, dxin, grads = one_sequence(pair[0], pair[1], norm_in, w_flat, conv_w, w_out, norm_mid, w_gate, w_up, w_down)
        return (jax.tree.map(lambda a, b: a + b, carry, grads), (out, dxin))
    totals, outs = lax.scan(step, zeros, (block_in, cot))
    return (outs[0], outs[1], totals[0], totals[1].reshape(D, 3, D), totals[2], totals[3], totals[4], totals[5], totals[6], totals[7])
```

```python
import functools

import jax
import jax.numpy as jnp
from jax import lax
from jax.experimental import pallas as pl
from jax.experimental.pallas import tpu as pltpu
from jax.sharding import PartitionSpec as P

EPS = 1e-05
BF = jnp.bfloat16
F32 = jnp.float32


def back_shift(arr, k):
    return jnp.concatenate([jnp.zeros((k, arr.shape[1]), F32), arr[:-k]], axis=0)


def fore_shift(arr, k):
    return jnp.concatenate([arr[k:], jnp.zeros((k, arr.shape[1]), F32)], axis=0)


def dot(a, b):
    return jnp.dot(a, b, preferred_element_type=F32)


def dot_t(a, b):
    return lax.dot_general(a, b, (((1,), (1,)), ((), ())), preferred_element_type=F32)


def t_dot(a, b):
    return lax.dot_general(a, b, (((0,), (0,)), ((), ())), preferred_element_type=F32)


def copy_body(index, src, dst):
    dst[...] = src[...]


def move_rows(arr, index):
    n = index.shape[0]
    rows, cols = arr.shape[0] // n, arr.shape[1]
    return pl.pallas_call(
        copy_body,
        grid_spec=pltpu.PrefetchScalarGridSpec(
            num_scalar_prefetch=1,
            grid=(n,),
            in_specs=[pl.BlockSpec((rows, cols), lambda k, ix: (ix[k], 0))],
            out_specs=pl.BlockSpec((rows, cols), lambda k, ix: (k, 0)),
        ),
        out_shape=jax.ShapeDtypeStruct(arr.shape, arr.dtype),
        cost_estimate=pl.CostEstimate(flops=0, bytes_accessed=2 * arr.size * arr.dtype.itemsize, transcendentals=0),
    )(index, arr)


def move_cols(arr, index):
    n = index.shape[0]
    rows, cols = arr.shape[0], arr.shape[1] // n
    return pl.pallas_call(
        copy_body,
        grid_spec=pltpu.PrefetchScalarGridSpec(
            num_scalar_prefetch=1,
            grid=(n,),
            in_specs=[pl.BlockSpec((rows, cols), lambda k, ix: (0, ix[k]))],
            out_specs=pl.BlockSpec((rows, cols), lambda k, ix: (0, k)),
        ),
        out_shape=jax.ShapeDtypeStruct(arr.shape, arr.dtype),
        cost_estimate=pl.CostEstimate(flops=0, bytes_accessed=2 * arr.size * arr.dtype.itemsize, transcendentals=0),
    )(index, arr)


def place_shares(arr, index):
    n, js, rows, cols = arr.shape
    return pl.pallas_call(
        copy_body,
        grid_spec=pltpu.PrefetchScalarGridSpec(
            num_scalar_prefetch=1,
            grid=(js, n),
            in_specs=[pl.BlockSpec((1, 1, rows, cols), lambda j, k, ix: (ix[k], j, 0, 0))],
            out_specs=pl.BlockSpec((1, 1, rows, cols), lambda j, k, ix: (j, k, 0, 0)),
        ),
        out_shape=jax.ShapeDtypeStruct((js, n, rows, cols), arr.dtype),
        cost_estimate=pl.CostEstimate(flops=0, bytes_accessed=2 * arr.size * arr.dtype.itemsize, transcendentals=0),
    )(index, arr)


def xor_blocks(blocks, by):
    blocks = list(blocks)
    bit = 1
    while bit < len(blocks):
        flip = (by & bit) != 0
        blocks = [jnp.where(flip, blocks[k ^ bit], blocks[k]) for k in range(len(blocks))]
        bit *= 2
    return blocks


def slot_order(bits):
    slots = [0]
    for b in reversed(bits):
        slots = slots + [e | (1 << b) for e in slots]
    return slots


def per_device(nd, nt, block_in, norm_in, w_in, conv_w, w_out, norm_mid, w_gate, w_up, w_down, cot):
    t = lax.axis_index("tensor")
    d = lax.axis_index("dp")
    width = block_in.shape[2]
    feats = w_in.shape[0]
    hidden = w_gate.shape[1]
    sub = nd // nt
    bits = list(range(nd.bit_length() - 1))
    order_one = bits
    order_two = bits[:1] + bits[2:3] + bits[1:2] + bits[3:]

    def over_tensor(arr, j):
        return lax.ppermute(arr, "tensor", [(i, i ^ j) for i in range(nt)])

    def over_dp(arr, e):
        return lax.ppermute(arr, "dp", [(i, i ^ e) for i in range(nd)])

    def gather(arr):
        return [over_tensor(arr, j) for j in range(1, nt)]

    def sum_dp(arr):
        for b in bits:
            arr = arr + over_dp(arr, 1 << b)
        return arr

    def slots_of(arr, order, by):
        step = arr.shape[1] // nd
        blocks = xor_blocks([arr[:, k * step : (k + 1) * step] for k in range(nd)], by)
        return jnp.concatenate([blocks[e] for e in slot_order(order)], axis=1)

    def halve(piece, size, order, axis):
        got = []
        for b in order:
            half = size // 2
            total = piece(half, size)
            for r in got:
                total = total + lax.slice_in_dim(r, half, size, axis=axis).astype(F32)
            new = over_dp(total.astype(BF), 1 << b)
            got = [lax.slice_in_dim(r, 0, half, axis=axis) for r in got] + [new]
            size = half
        total = piece(0, size)
        for r in got:
            total = total + r.astype(F32)
        return total

    around = t ^ jnp.arange(nt, dtype=jnp.int32)
    by = d ^ (sub * t)

    def gains(vec):
        return xor_blocks([vec[k * width : (k + 1) * width][None] for k in range(nt)], t)

    x_own = block_in[0]
    gy_own = cot[0]
    gain_one = gains(norm_in)
    gain_two = gains(norm_mid)
    x0 = (x_own * gain_one[0]).astype(BF)
    xs = gather(x0)

    w_in_r = move_rows(w_in.reshape(feats, 3 * width), around)
    wg_r = move_rows(w_gate, around)
    wu_r = move_rows(w_up, around)
    wd_r = move_cols(w_down, around)
    wo_r = move_cols(w_out, around)

    share = width // nd
    part = lax.dynamic_slice_in_dim(wo_r, d * share, share, axis=0)
    shares = []
    for j in range(1, nt):
        cols = [part[:, (j ^ k) * width : ((j ^ k) + 1) * width] for k in range(nt)]
        shares.append(over_tensor(jnp.concatenate(cols, axis=1), j))
    held = jnp.stack(shares)[None]
    if bits:
        held = jnp.concatenate([held, over_dp(held, 1)], axis=0)
    if nd == 8:
        held = jnp.concatenate([held] + [over_dp(held, e) for e in (2, 4, 6)], axis=0)
    else:
        for b in bits[1:]:
            held = jnp.concatenate([held, over_dp(held, 1 << b)], axis=0)
    wo_others = place_shares(held, d ^ jnp.arange(nd, dtype=jnp.int32)).reshape((nt - 1) * width, feats)

    x_others = jnp.concatenate(xs, axis=1)
    gain_one_all = jnp.concatenate(gain_one, axis=1)
    gain_two_all = jnp.concatenate(gain_two, axis=1)
    xf_others = x_others.astype(F32) / gain_one_all[:, width:]
    sq = jnp.sum(x_own * x_own, axis=1, keepdims=True) + jnp.sum(xf_others * xf_others, axis=1, keepdims=True)
    q1 = lax.rsqrt(sq / feats + EPS)
    proj = (dot(x0, w_in_r[:width]) + dot(x_others, w_in_r[width:])) * q1
    bgate = proj[:, :width]
    cgate = proj[:, width : 2 * width]
    xval = proj[:, 2 * width :]
    vmix = bgate * xval
    conv = conv_w[0] * vmix + conv_w[1] * back_shift(vmix, 1) + conv_w[2] * back_shift(vmix, 2)
    zmix = (cgate * conv).astype(BF)

    zs = gather(zmix)
    z_others = jnp.concatenate(zs, axis=1)
    x_full = jnp.concatenate([x_own, xf_others], axis=1)
    resid = x_full + (dot(zmix, wo_r) + dot(z_others, wo_others))
    r_own = resid[:, :width]
    q2 = lax.rsqrt(jnp.mean(resid * resid, axis=1, keepdims=True) + EPS)
    n2 = resid * q2
    h2 = (n2 * gain_two_all).astype(BF)
    n2b = n2.astype(BF)

    c0, z_held = lax.optimization_barrier((gy_own.astype(BF), z_others[:8, :128]))
    cs = gather(c0)

    gpre = dot(h2, wg_r)
    upre = dot(h2, wu_r)
    sg = jax.nn.sigmoid(gpre)
    act = (gpre * sg * upre).astype(BF)
    outs = [over_tensor(dot(act, wd_r[:, j * width : (j + 1) * width]).astype(BF), j) for j in range(1, nt)]
    out_own = r_own + dot(act, wd_r[:, :width])
    for r in outs:
        out_own = out_own + r.astype(F32)

    cotb = jnp.concatenate([c0] + cs, axis=1)
    dact = dot_t(cotb, wd_r)
    dgate = (dact * upre * sg * (1.0 + gpre * (1.0 - sg))).astype(BF)
    dup = (dact * gpre * sg).astype(BF)

    e2 = ((dot_t(dgate, wg_r) + dot_t(dup, wu_r)) * gain_two_all * q2).astype(BF)
    wo_j = [wo_others[j * width : (j + 1) * width] for j in range(nt - 1)]
    zgs = [over_tensor(dot_t(e2, wo_j[j - 1]).astype(BF), j) for j in range(1, nt)]
    dot_two = jnp.sum(dgate.astype(F32) * gpre + dup.astype(F32) * upre, axis=1)
    dots_two = gather(dot_two)
    for r in dots_two:
        dot_two = dot_two + r
    mean_two = (dot_two / feats)[:, None] * q2
    dz = dot_t(cotb, wo_r) + dot_t(e2, wo_r) - mean_two * dot_t(n2b, wo_r)
    for r in zgs:
        dz = dz + r.astype(F32)

    e2_held, zg_held = lax.optimization_barrier((e2, zgs[-1][:8, :128]))
    e2s = [over_tensor(e2_held[:, j * width : (j + 1) * width], j) for j in range(1, nt)]

    h2_one = slots_of(h2, order_one, by)
    h2_two = slots_of(h2, order_two, by)
    cot_one = slots_of(cotb, order_one, by)
    s_down = halve(lambda lo, hi: t_dot(act, cot_one[:, lo:hi]), feats, order_one, 1)
    s_gate = halve(lambda lo, hi: t_dot(h2_one[:, lo:hi], dgate), feats, order_one, 0)
    s_up = halve(lambda lo, hi: t_dot(h2_two[:, lo:hi], dup), feats, order_two, 0)

    dcg = dz * conv
    dconv = dz * cgate
    g_conv = [
        jnp.sum(dconv * vmix, axis=0),
        jnp.sum(dconv * back_shift(vmix, 1), axis=0),
        jnp.sum(dconv * back_shift(vmix, 2), axis=0),
    ]
    dv = conv_w[0] * dconv + conv_w[1] * fore_shift(dconv, 1) + conv_w[2] * fore_shift(dconv, 2)
    dproj = (jnp.concatenate([dv * xval, dcg, dv * bgate], axis=1) * q1).astype(BF)
    dh_list = [dot_t(dproj, w_in_r[j * width : (j + 1) * width]).astype(BF) for j in range(1, nt)]
    dhs = [over_tensor(dh_list[j - 1], j) for j in range(1, nt)]
    dh_mine = dot_t(dproj, w_in_r[:width])
    dot_one = jnp.sum(dproj.astype(F32) * proj, axis=1)
    for r in gather(dot_one):
        dot_one = dot_one + r

    half = (3 * width) // 2
    x_all = jnp.concatenate([x0, x_others], axis=1)
    x_one = slots_of(x_all, order_one, by)
    x_two = slots_of(x_all, order_two, by)
    s_in = jnp.concatenate(
        [
            halve(lambda lo, hi: t_dot(x_one[:, lo:hi], dproj[:, :half]), feats, order_one, 0),
            halve(lambda lo, hi: t_dot(x_two[:, lo:hi], dproj[:, half:]), feats, order_two, 0),
        ],
        axis=1,
    ).reshape(feats // nd, 3, width)

    g_norm = jnp.sum(dh_mine * x_own, axis=0)
    for j in range(1, nt):
        v = jnp.sum(dh_list[j - 1].astype(F32) * xf_others[:, (j - 1) * width : j * width], axis=0)
        g_norm = g_norm + over_tensor(v, j)
    s_norm = sum_dp(g_norm)

    e2_own = e2[:, :width].astype(F32)
    for r in e2s:
        e2_own = e2_own + r.astype(F32)
    dres = gy_own + e2_own - r_own * q2 * mean_two
    g_mid = jnp.sum(e2_own * r_own, axis=0) / gain_two[0][0]
    small = sum_dp(jnp.stack(g_conv + [g_mid]))

    dresb = dres.astype(BF)
    z_all = jnp.concatenate([zmix, z_others], axis=1)
    fine = width // sub
    dres_u = xor_blocks([dresb[:, u * fine : (u + 1) * fine] for u in range(sub)], d & (sub - 1))
    z_j = xor_blocks([zmix] + zs, d // sub)
    order_out = bits
    slots = slot_order(order_out)

    def out_piece(lo, hi):
        rows = [t_dot(z_j[e // sub], dres_u[e % sub]) for e in slots[lo:hi]]
        return jnp.concatenate(rows, axis=0) if len(rows) > 1 else rows[0]

    got = []
    size = nd
    for b in order_out:
        mid = size // 2
        total = out_piece(mid, size)
        for r in got:
            total = total + r[mid * width : size * width].astype(F32)
        new = over_dp(total.astype(BF), 1 << b)
        got = [r[: mid * width] for r in got] + [new]
        size = mid
    piece = out_piece(0, 1)
    for r in got:
        piece = piece + r.astype(F32)
    home = [
        (a * nt + b, (sub * b + a % sub) * nt + (b ^ (a // sub))) for a in range(nd) for b in range(nt)
    ]
    s_out = lax.ppermute(piece.astype(BF), ("dp", "tensor"), home).astype(F32)

    dh_own = dh_mine
    for r in dhs:
        dh_own = dh_own + r.astype(F32)
    dx = dres + dh_own * gain_one[0] - x_own * (q1 * (dot_one / feats)[:, None])
    return (
        out_own[None],
        dx[None],
        s_norm,
        s_in,
        small[:3],
        s_out,
        small[3],
        s_gate,
        s_up,
        s_down,
    )


def solution(mesh):
    placed = (
        P("dp", None, "tensor"),
        P(),
        P(None, None, "tensor"),
        P(None, "tensor"),
        P("tensor", None),
        P(),
        P(None, "tensor"),
        P(None, "tensor"),
        P("tensor", None),
        P("dp", None, "tensor"),
    )
    return jax.shard_map(
        functools.partial(per_device, mesh.shape["dp"], mesh.shape["tensor"]),
        mesh=mesh,
        in_specs=placed,
        out_specs=(
            P("dp", None, "tensor"),
            P("dp", None, "tensor"),
            P("tensor"),
            P("dp", None, "tensor"),
            P(None, "tensor"),
            P("tensor", "dp"),
            P("tensor"),
            P("dp", "tensor"),
            P("dp", "tensor"),
            P("tensor", "dp"),
        ),
        check_vma=False,
    )
```

```python
import functools

import jax
import jax.numpy as jnp
from jax import lax
from jax.experimental import pallas as pl
from jax.experimental.pallas import tpu as pltpu
from jax.sharding import PartitionSpec as P

EPS = 1e-05
BF = jnp.bfloat16
F32 = jnp.float32
ANY = pl.BlockSpec(memory_space=pl.ANY)
SMEM = pl.BlockSpec(memory_space=pltpu.SMEM)
VMEM = pl.BlockSpec(memory_space=pltpu.VMEM)


def dot(a, b):
    return jnp.dot(a, b, preferred_element_type=F32)


def dot_t(a, b):
    return lax.dot_general(a, b, (((1,), (1,)), ((), ())), preferred_element_type=F32)


def shape(dims, kind):
    return jax.ShapeDtypeStruct(tuple(dims), kind)


def call(body, args, specs, outs, scratch, flops, name):
    total = sum(a.size * a.dtype.itemsize for a in args) + sum(o.size * o.dtype.itemsize for o in outs)
    return pl.pallas_call(
        body,
        in_specs=specs,
        out_specs=[VMEM] * len(outs),
        out_shape=outs,
        scratch_shapes=scratch,
        cost_estimate=pl.CostEstimate(flops=int(flops), bytes_accessed=int(total), transcendentals=0),
        compiler_params=pltpu.CompilerParams(vmem_limit_bytes=56 * 1024 * 1024),
        name=name,
    )(*args)


def rows_at(index, size):
    return pl.ds(pl.multiple_of(index * size, size), size)


def back(arr, k):
    place = lax.broadcasted_iota(jnp.int32, arr.shape, 0)
    return jnp.where(place >= k, pltpu.roll(arr, k, 0), 0.0)


def fore(arr, k):
    place = lax.broadcasted_iota(jnp.int32, arr.shape, 0)
    return jnp.where(place < arr.shape[0] - k, pltpu.roll(arr, arr.shape[0] - k, 0), 0.0)


def tile_of(size):
    for tile in (384, 256, 128):
        if size % tile == 0:
            return tile
    return size


def mixer_body(nt, idx, *refs):
    x_own = refs[0]
    xs = refs[1 : 1 + nt]
    norm, w_hbm, taps, zmix, proj, conv, q1_ref, w, sem = refs[1 + nt :]
    load = pltpu.make_async_copy(w_hbm, w, sem)
    load.start()
    t = idx[0]
    width = x_own.shape[1]
    x = x_own[...]
    sq = jnp.sum(x * x, axis=1, keepdims=True)
    for j in range(1, nt):
        v = xs[j][...].astype(F32) / norm[pl.ds(t ^ j, 1), :]
        sq = sq + jnp.sum(v * v, axis=1, keepdims=True)
    q1 = lax.rsqrt(sq / (nt * width) + EPS)
    q1_ref[...] = q1
    load.wait()
    total = dot(xs[0][...], w[rows_at(t, width), :])
    for j in range(1, nt):
        total = total + dot(xs[j][...], w[rows_at(t ^ j, width), :])
    total = total * q1
    proj[...] = total
    bgate = total[:, :width]
    cgate = total[:, width : 2 * width]
    vmix = bgate * total[:, 2 * width :]
    cv = taps[0:1, :] * vmix + taps[1:2, :] * back(vmix, 1) + taps[2:3, :] * back(vmix, 2)
    conv[...] = cv
    zmix[...] = (cgate * cv).astype(BF)


def start_mixer_weights(d, groups, held, own_hbm, own, wo, sems):
    loads = [pltpu.make_async_copy(own_hbm, own, sems.at[0])]
    for group, (ref, es) in enumerate(zip(held, groups)):
        for at, e in enumerate(es):
            share = ref.shape[2]
            loads.append(
                pltpu.make_async_copy(
                    ref.at[at], wo.at[:, rows_at(d ^ e, share), :], sems.at[1 + e]
                )
            )
    for load in loads:
        load.start()
    return loads


def forward_body(nt, groups, idx, *refs):
    refs = list(refs)

    def take(n):
        got, refs[:n] = refs[:n], []
        return got

    (x_own,) = take(1)
    xs = take(nt - 1)
    norm_one, norm_two = take(2)
    zs = take(nt)
    (own_hbm,) = take(1)
    held = take(len(groups))
    wg_hbm, wu_hbm, wd_hbm = take(3)
    resid, q2_ref, h2, gpre, upre, act, out_own = take(7)
    outs = take(nt - 1)
    own, wo, wg, wu, wd, sems, wsems = take(7)
    t, d = idx[0], idx[1]
    loads = start_mixer_weights(d, groups, held, own_hbm, own, wo, sems)
    big = [pltpu.make_async_copy(a, b, wsems.at[i]) for i, (a, b) in enumerate(((wg_hbm, wg), (wu_hbm, wu), (wd_hbm, wd)))]
    for b in big:
        b.start()
    width = x_own.shape[1]
    for load in loads:
        load.wait()
    sq = 0.0
    for k in range(nt):
        cols = rows_at(t ^ k, width)
        x = x_own[...] if k == 0 else xs[k - 1][...].astype(F32) / norm_one[pl.ds(t ^ k, 1), :]
        mixed = dot(zs[0][...], own[:, cols])
        for j in range(1, nt):
            mixed = mixed + dot(zs[j][...], wo[j - 1, :, cols])
        r = x + mixed
        resid[:, k * width : (k + 1) * width] = r
        sq = sq + jnp.sum(r * r, axis=1, keepdims=True)
    q2 = lax.rsqrt(sq / (nt * width) + EPS)
    q2_ref[...] = q2
    for k in range(nt):
        r = resid[:, k * width : (k + 1) * width]
        h2[:, k * width : (k + 1) * width] = (r * q2 * norm_two[pl.ds(t ^ k, 1), :]).astype(BF)
    big[0].wait()
    big[1].wait()
    hidden = gpre.shape[1]
    tile = tile_of(hidden)

    @pl.loop(0, hidden // tile)
    def _(i):
        cols = rows_at(i, tile)
        g = u = 0.0
        for k in range(nt):
            h = h2[:, k * width : (k + 1) * width]
            g = g + dot(h, wg[rows_at(t ^ k, width), cols])
            u = u + dot(h, wu[rows_at(t ^ k, width), cols])
        gpre[:, cols] = g
        upre[:, cols] = u
        act[:, cols] = (g * jax.nn.sigmoid(g) * u).astype(BF)

    big[2].wait()
    out_own[...] = resid[:, :width] + dot(act[...], wd[:, rows_at(t, width)])
    for j in range(1, nt):
        outs[j - 1][...] = dot(act[...], wd[:, rows_at(t ^ j, width)]).astype(BF)


def backward_body(nt, groups, idx, *refs):
    refs = list(refs)

    def take(n):
        got, refs[:n] = refs[:n], []
        return got

    cs = take(nt)
    (norm_two,) = take(1)
    resid, q2_ref, gpre, upre = take(4)
    (own_hbm,) = take(1)
    held = take(len(groups))
    wg_hbm, wu_hbm, wd_hbm = take(3)
    dgate, dup, dz, mids = take(4)
    es = take(nt)
    zgs = take(nt - 1)
    own, wo, wg, wu, wd, sems, wsems = take(7)
    t, d = idx[0], idx[1]
    big = [pltpu.make_async_copy(a, b, wsems.at[i]) for i, (a, b) in enumerate(((wd_hbm, wd), (wg_hbm, wg), (wu_hbm, wu)))]
    for b in big:
        b.start()
    loads = start_mixer_weights(d, groups, held, own_hbm, own, wo, sems)
    width = cs[0].shape[1]
    hidden = gpre.shape[1]
    tile = tile_of(hidden)
    big[0].wait()

    def step(i, total):
        cols = rows_at(i, tile)
        dact = 0.0
        for k in range(nt):
            dact = dact + dot_t(cs[k][...], wd[cols, rows_at(t ^ k, width)])
        g = gpre[:, cols]
        u = upre[:, cols]
        sg = jax.nn.sigmoid(g)
        dg = (dact * u * sg * (1.0 + g * (1.0 - sg))).astype(BF)
        du = (dact * g * sg).astype(BF)
        dgate[:, cols] = dg
        dup[:, cols] = du
        return total + jnp.sum(dg.astype(F32) * g + du.astype(F32) * u, axis=1, keepdims=True)

    total = lax.fori_loop(0, hidden // tile, step, jnp.zeros((cs[0].shape[0], 1), F32))
    q2 = q2_ref[...]
    mean = total * q2 / (nt * width)
    big[1].wait()
    big[2].wait()
    for j in range(nt):
        rows = rows_at(t ^ j, width)
        dh = dot_t(dgate[...], wg[rows, :]) + dot_t(dup[...], wu[rows, :])
        n = resid[:, j * width : (j + 1) * width] * q2
        mids[j : j + 1, :] = jnp.sum(dh * n, axis=0, keepdims=True)
        es[j][...] = (q2 * (dh * norm_two[pl.ds(t ^ j, 1), :]) - n * mean).astype(BF)
    for load in loads:
        load.wait()
    for j in range(1, nt):
        zg = 0.0
        for k in range(nt):
            zg = zg + dot_t(es[k][...], wo[j - 1, :, rows_at(t ^ k, width)])
        zgs[j - 1][...] = zg.astype(BF)
    mine = 0.0
    for k in range(nt):
        part = own[:, rows_at(t ^ k, width)]
        mine = mine + dot_t(es[k][...], part) + dot_t(cs[k][...], part)
    dz[...] = mine


def mixer_back_body(nt, idx, *refs):
    refs = list(refs)

    def take(n):
        got, refs[:n] = refs[:n], []
        return got

    (dz_ref,) = take(1)
    zgs = take(nt - 1)
    x_own, proj, conv, q1_ref, norm, mids, taps = take(7)
    xs = take(nt - 1)
    (w_hbm,) = take(1)
    dproj, u_own = take(2)
    us = take(nt - 1)
    vecs = take(nt)
    w, sem = take(2)
    load = pltpu.make_async_copy(w_hbm, w, sem)
    load.start()
    t = idx[0]
    width = x_own.shape[1]
    dz = dz_ref[...]
    for r in zgs:
        dz = dz + r[...].astype(F32)
    q1 = q1_ref[...]
    bgate = proj[:, :width]
    cgate = proj[:, width : 2 * width]
    xval = proj[:, 2 * width :]
    vmix = bgate * xval
    dcg = dz * conv[...]
    dconv = dz * cgate
    vecs[0][...] = jnp.zeros(vecs[0].shape, F32)
    vecs[0][0:1, :] = jnp.sum(dconv * vmix, axis=0, keepdims=True)
    vecs[0][1:2, :] = jnp.sum(dconv * back(vmix, 1), axis=0, keepdims=True)
    vecs[0][2:3, :] = jnp.sum(dconv * back(vmix, 2), axis=0, keepdims=True)
    dv = taps[0:1, :] * dconv + taps[1:2, :] * fore(dconv, 1) + taps[2:3, :] * fore(dconv, 2)
    total = 0.0
    for at, value, saved in ((0, dv * xval, bgate), (1, dcg, cgate), (2, dv * bgate, xval)):
        value = (value * q1).astype(BF)
        dproj[:, at * width : (at + 1) * width] = value
        total = total + jnp.sum(value.astype(F32) * saved, axis=1, keepdims=True)
    mean = total * q1 / (nt * width)
    load.wait()
    for j in range(nt):
        gain = norm[pl.ds(t ^ j, 1), :]
        x = x_own[...] if j == 0 else xs[j - 1][...].astype(F32) / gain
        dh = dot_t(dproj[...], w[rows_at(t ^ j, width), :])
        u = dh * gain - x * mean
        if j == 0:
            u_own[...] = u
        else:
            us[j - 1][...] = u.astype(BF)
            vecs[j][...] = jnp.zeros(vecs[j].shape, F32)
        vecs[j][3:4, :] = mids[j : j + 1, :]
        vecs[j][4:5, :] = jnp.sum(dh * x, axis=0, keepdims=True)


def turn_body(nt, *refs):
    out = refs[-1]
    for j in range(nt):
        width = refs[j].shape[1]
        out[j * width : (j + 1) * width, :] = refs[j][...].astype(F32).T.astype(BF)


def turn(blocks):
    rows, width = blocks[0].shape
    return call(
        functools.partial(turn_body, len(blocks)),
        blocks, [VMEM] * len(blocks), [shape((width * len(blocks), rows), BF)], [], 0, "turn",
    )[0]


def slot_order(bits):
    slots = [0]
    for b in reversed(bits):
        slots = slots + [e | (1 << b) for e in slots]
    return slots


def grad_stage(idx, a, streams, step, kind):
    plan, args, outs, flops = [], [idx, a], [], 0
    for b, slots, got in streams:
        plan.append((tuple((e, tuple(lows)) for e, lows in slots), len(got)))
        args.append(b)
        args.extend(got)
        outs.append(shape((len(slots) * step, b.shape[1]), kind))
        flops += 2 * len(slots) * step * b.size
    return call(functools.partial(stage_body, tuple(plan), step), args, [SMEM] + [VMEM] * (len(args) - 1), outs, [], flops, "grads")


def stage_body(plan, step, idx, a, *refs):
    refs = list(refs)
    by = idx[2]
    ins = []
    for slots, n_got in plan:
        b = refs.pop(0)
        ins.append((slots, b, [refs.pop(0) for _ in range(n_got)]))
    for slots, b, got in ins:
        out = refs.pop(0)
        for at, (e, lows) in enumerate(slots):
            value = dot(a[rows_at(e ^ by, step), :], b[...])
            for r, low in zip(got, lows):
                value = value + r[low * step : (low + 1) * step, :].astype(F32)
            out[at * step : (at + 1) * step, :] = value.astype(out.dtype)


def mix_grad_body(plan, sub, step, idx, dres, *refs):
    slots, n_z, n_got = plan
    zs = refs[:n_z]
    got = refs[n_z : n_z + n_got]
    out, turned, held = refs[n_z + n_got :]
    d = idx[1]
    turned[...] = dres[...].T.astype(BF)
    for j in range(n_z):
        held[j] = zs[j][...]
    for at, (e, lows) in enumerate(slots):
        a = turned[rows_at((e % sub) ^ (d & (sub - 1)), step), :]
        value = dot(a, held[(e // sub) ^ (d // sub)])
        for r, low in zip(got, lows):
            value = value + r[low * step : (low + 1) * step, :].astype(F32)
        out[at * step : (at + 1) * step, :] = value.astype(out.dtype)


def per_device(nd, nt, block_in, norm_in, w_in, conv_w, w_out, norm_mid, w_gate, w_up, w_down, cot):
    t = lax.axis_index("tensor")
    d = lax.axis_index("dp")
    rows, width = block_in.shape[1:]
    feats = w_in.shape[0]
    hidden = w_gate.shape[1]
    sub = nd // nt
    step = feats // nd
    bits = list(range(nd.bit_length() - 1))
    order_one = bits
    order_two = bits[:1] + bits[2:3] + bits[1:2] + bits[3:]
    idx = jnp.stack([t, d, d ^ (sub * t)]).astype(jnp.int32)

    def over_tensor(arr, j):
        return lax.ppermute(arr, "tensor", [(i, i ^ j) for i in range(nt)])

    def over_dp(arr, e):
        return lax.ppermute(arr, "dp", [(i, i ^ e) for i in range(nd)])

    def gather(arr):
        return [over_tensor(arr, j) for j in range(1, nt)]

    def halve(order):
        slots = slot_order(order)
        got = []
        for b in order:
            mid = len(slots) // 2
            sent = yield [(slots[p], [p] * len(got)) for p in range(mid, len(slots))], got
            got = got + [over_dp(sent, 1 << b)]
            slots = slots[:mid]
        yield [(slots[0], [0] * len(got))], got

    def run(streams, call_one):
        gens = [halve(order) for order in streams]
        asks = [next(g) for g in gens]
        for _ in range(len(bits)):
            sent = call_one(asks, BF)
            asks = [g.send(s) for g, s in zip(gens, sent)]
        return call_one(asks, F32)

    gain_one = norm_in.reshape(nt, width)
    gain_two = norm_mid.reshape(nt, width)
    x_own = block_in[0]
    gy_own = cot[0]
    x0 = (x_own * lax.dynamic_slice_in_dim(gain_one, t, 1, axis=0)).astype(BF)
    xs = gather(x0)
    w_flat = w_in.reshape(feats, 3 * width)

    share = width // nd
    part = lax.dynamic_slice_in_dim(w_out, d * share, share, axis=0)
    held = [jnp.stack(gather(part))[None]]
    groups = [[0]]
    held.append(over_dp(held[0], 1))
    groups.append([1])
    if nd == 8:
        pair = jnp.concatenate(held, axis=0)
        for e in (2, 4, 6):
            held.append(over_dp(pair, e))
            groups.append([e, e + 1])
    else:
        for b in bits[1:]:
            whole = jnp.concatenate(held, axis=0)
            held.append(over_dp(whole, 1 << b))
            groups.append([e | (1 << b) for e in range(1 << b)])
    groups = tuple(tuple(g) for g in groups)

    zmix, proj, conv, q1 = call(
        functools.partial(mixer_body, nt),
        [idx, x_own, x0] + xs + [gain_one, w_flat, conv_w],
        [SMEM] + [VMEM] * (2 + nt) + [ANY, VMEM],
        [shape((rows, width), BF), shape((rows, 3 * width), F32), shape((rows, width), F32), shape((rows, 1), F32)],
        [pltpu.VMEM((feats, 3 * width), BF), pltpu.SemaphoreType.DMA],
        2 * rows * w_flat.size,
        "mixer",
    )
    zs = gather(zmix)
    c0 = gy_own.astype(BF)
    cs = [c0] + gather(c0)

    weights = [
        pltpu.VMEM((width, feats), BF),
        pltpu.VMEM((nt - 1, width, feats), BF),
        pltpu.VMEM((feats, hidden), BF),
        pltpu.VMEM((feats, hidden), BF),
        pltpu.VMEM((hidden, feats), BF),
        pltpu.SemaphoreType.DMA((1 + nd,)),
        pltpu.SemaphoreType.DMA((3,)),
    ]
    block = shape((rows, width), BF)
    blockf = shape((rows, width), F32)
    wide = shape((rows, hidden), F32)
    wideb = shape((rows, hidden), BF)
    resid, q2, h2, gpre, upre, act, out_own, *outs = call(
        functools.partial(forward_body, nt, groups),
        [idx, x_own] + xs + [gain_one, gain_two, zmix] + zs + [w_out] + held + [w_gate, w_up, w_down],
        [SMEM] + [VMEM] * (nt + 2 + nt) + [ANY] * (1 + len(held) + 3),
        [shape((rows, feats), F32), shape((rows, 1), F32), shape((rows, feats), BF), wide, wide, wideb, blockf]
        + [block] * (nt - 1),
        weights,
        2 * rows * (feats * feats + 3 * feats * hidden),
        "forward",
    )
    for o in outs_of(outs, over_tensor):
        out_own = out_own + o.astype(F32)

    dgate, dup, dz, mids, *rest = call(
        functools.partial(backward_body, nt, groups),
        [idx] + cs + [gain_two, resid, q2, gpre, upre, w_out] + held + [w_gate, w_up, w_down],
        [SMEM] + [VMEM] * (nt + 5) + [ANY] * (1 + len(held) + 3),
        [wideb, wideb, blockf, shape((nt, width), F32)] + [block] * nt + [block] * (nt - 1),
        weights,
        2 * rows * (2 * feats * feats + 3 * feats * hidden),
        "backward",
    )
    es, zgs = rest[:nt], rest[nt:]
    zgs = outs_of(zgs, over_tensor)
    e_got = outs_of(es[1:], over_tensor)

    h2_t = turn([h2])
    cot_t = turn(cs)

    def on(a, bs):
        def one(asks, kind):
            streams = [(b, slots, got) for b, (slots, got) in zip(bs, asks)]
            return grad_stage(idx, a, streams, step, kind)

        return one

    (s_down,) = run([order_two], on(cot_t, [act]))
    s_gate, s_up = run([order_one, order_two], on(h2_t, [dgate, dup]))

    vec = shape((8, width), F32)
    dproj, u_own, *rest = call(
        functools.partial(mixer_back_body, nt),
        [idx, dz] + zgs + [x_own, proj, conv, q1, gain_one, mids, conv_w] + xs + [w_flat],
        [SMEM] + [VMEM] * (1 + (nt - 1) + 7 + (nt - 1)) + [ANY],
        [shape((rows, 3 * width), BF), blockf] + [block] * (nt - 1) + [vec] * nt,
        [pltpu.VMEM((feats, 3 * width), BF), pltpu.SemaphoreType.DMA],
        2 * rows * w_flat.size,
        "mixer_back",
    )
    us, vecs = rest[: nt - 1], rest[nt - 1 :]
    us = outs_of(us, over_tensor)
    small = vecs[0]
    for v in outs_of(vecs[1:], over_tensor):
        small = small + v
    for b in bits:
        small = small + over_dp(small, 1 << b)
    x_t = turn([x0] + xs)
    (s_in,) = run([order_one], on(x_t, [dproj]))

    dres = gy_own + es[0].astype(F32)
    for r in e_got:
        dres = dres + r.astype(F32)

    fine = width // sub

    def mix_grads(asks, kind):
        slots, got = asks[0]
        plan = (tuple((e, tuple(lows)) for e, lows in slots), nt, len(got))
        return call(
            functools.partial(mix_grad_body, plan, sub, fine),
            [idx, dres, zmix] + zs + got,
            [SMEM] + [VMEM] * (1 + nt + len(got)),
            [shape((len(slots) * fine, width), kind)],
            [pltpu.VMEM((width, rows), BF), pltpu.VMEM((nt, rows, width), BF)],
            2 * rows * width * fine * len(slots),
            "mix_grads",
        )

    (piece,) = run([order_two], mix_grads)
    home = [
        (a * nt + b, (sub * b + a % sub) * nt + (b ^ (a // sub))) for a in range(nd) for b in range(nt)
    ]
    s_out = lax.ppermute(piece.astype(BF), ("dp", "tensor"), home).astype(F32).T

    dx = dres + u_own
    for r in us:
        dx = dx + r.astype(F32)
    return (
        out_own[None],
        dx[None],
        small[4],
        s_in.reshape(step, 3, width),
        small[:3],
        s_out,
        small[3],
        s_gate,
        s_up,
        s_down.T,
    )


def outs_of(arrs, over_tensor):
    return [over_tensor(a, j + 1) for j, a in enumerate(arrs)]


def solution(mesh):
    placed = (
        P("dp", None, "tensor"),
        P(),
        P(None, None, "tensor"),
        P(None, "tensor"),
        P("tensor", None),
        P(),
        P(None, "tensor"),
        P(None, "tensor"),
        P("tensor", None),
        P("dp", None, "tensor"),
    )
    return jax.shard_map(
        functools.partial(per_device, mesh.shape["dp"], mesh.shape["tensor"]),
        mesh=mesh,
        in_specs=placed,
        out_specs=(
            P("dp", None, "tensor"),
            P("dp", None, "tensor"),
            P("tensor"),
            P("dp", None, "tensor"),
            P(None, "tensor"),
            P("tensor", "dp"),
            P("tensor"),
            P("dp", "tensor"),
            P("dp", "tensor"),
            P("tensor", "dp"),
        ),
        check_vma=False,
    )
```

```python
import functools

import jax
import jax.numpy as jnp
from jax import lax
from jax.experimental import pallas as pl
from jax.experimental.pallas import tpu as pltpu
from jax.sharding import PartitionSpec as P

EPS = 1e-05
BF = jnp.bfloat16
F32 = jnp.float32
ANY = pl.BlockSpec(memory_space=pl.ANY)
SMEM = pl.BlockSpec(memory_space=pltpu.SMEM)
VMEM = pl.BlockSpec(memory_space=pltpu.VMEM)


def dot(a, b):
    return jnp.dot(a, b, preferred_element_type=F32)


def dot_t(a, b):
    return lax.dot_general(a, b, (((1,), (1,)), ((), ())), preferred_element_type=F32)


def shape(dims, kind):
    return jax.ShapeDtypeStruct(tuple(dims), kind)


def call(body, args, specs, outs, scratch, flops, vmem=40):
    total = sum(a.size * a.dtype.itemsize for a in args) + sum(o.size * o.dtype.itemsize for o in outs)
    return pl.pallas_call(
        body,
        in_specs=specs,
        out_specs=[VMEM] * len(outs),
        out_shape=outs,
        scratch_shapes=scratch,
        cost_estimate=pl.CostEstimate(flops=int(flops), bytes_accessed=int(total), transcendentals=0),
        compiler_params=pltpu.CompilerParams(vmem_limit_bytes=vmem * 1024 * 1024),
    )(*args)


def rows_at(index, size):
    return pl.ds(pl.multiple_of(index * size, size), size)


def back(arr, k):
    place = lax.broadcasted_iota(jnp.int32, arr.shape, 0)
    return jnp.where(place >= k, pltpu.roll(arr, k, 0), 0.0)


def fore(arr, k):
    place = lax.broadcasted_iota(jnp.int32, arr.shape, 0)
    return jnp.where(place < arr.shape[0] - k, pltpu.roll(arr, arr.shape[0] - k, 0), 0.0)


def tile_of(size):
    for tile in (384, 256, 128):
        if size % tile == 0:
            return tile
    return size


def mixer_body(nt, idx, *refs):
    x_own = refs[0]
    xs = refs[1 : 1 + nt]
    norm, w_hbm, taps, zmix, proj, conv, q1_ref, w, sem = refs[1 + nt :]
    load = pltpu.make_async_copy(w_hbm, w, sem)
    load.start()
    t = idx[0]
    width = x_own.shape[1]
    x = x_own[...]
    sq = jnp.sum(x * x, axis=1, keepdims=True)
    for j in range(1, nt):
        v = xs[j][...].astype(F32) / norm[pl.ds(t ^ j, 1), :]
        sq = sq + jnp.sum(v * v, axis=1, keepdims=True)
    q1 = lax.rsqrt(sq / (nt * width) + EPS)
    q1_ref[...] = q1
    load.wait()
    total = dot(xs[0][...], w[rows_at(t, width), :])
    for j in range(1, nt):
        total = total + dot(xs[j][...], w[rows_at(t ^ j, width), :])
    total = total * q1
    proj[...] = total
    bgate = total[:, :width]
    cgate = total[:, width : 2 * width]
    vmix = bgate * total[:, 2 * width :]
    cv = taps[0:1, :] * vmix + taps[1:2, :] * back(vmix, 1) + taps[2:3, :] * back(vmix, 2)
    conv[...] = cv
    zmix[...] = (cgate * cv).astype(BF)


def start_mixer_weights(d, groups, held, own_hbm, own, wo, sems):
    loads = [pltpu.make_async_copy(own_hbm, own, sems.at[0])]
    for ref, es in zip(held, groups):
        for at, e in enumerate(es):
            share = ref.shape[2]
            loads.append(
                pltpu.make_async_copy(
                    ref.at[at], wo.at[:, rows_at(d ^ e, share), :], sems.at[1 + e]
                )
            )
    for load in loads:
        load.start()
    return loads


def forward_body(nt, groups, idx, *refs):
    refs = list(refs)

    def take(n):
        got, refs[:n] = refs[:n], []
        return got

    (x_own,) = take(1)
    xs = take(nt - 1)
    norm_one, norm_two = take(2)
    zs = take(nt)
    (own_hbm,) = take(1)
    held = take(len(groups))
    wg_hbm, wu_hbm = take(2)
    resid, q2_ref, h2, gpre, upre, act = take(6)
    own, wo, wg, wu, sems, wsems = take(6)
    t, d = idx[0], idx[1]
    loads = start_mixer_weights(d, groups, held, own_hbm, own, wo, sems)
    big = [pltpu.make_async_copy(a, b, wsems.at[i]) for i, (a, b) in enumerate(((wg_hbm, wg), (wu_hbm, wu)))]
    for b in big:
        b.start()
    width = x_own.shape[1]
    for load in loads:
        load.wait()
    sq = 0.0
    for k in range(nt):
        cols = rows_at(t ^ k, width)
        x = x_own[...] if k == 0 else xs[k - 1][...].astype(F32) / norm_one[pl.ds(t ^ k, 1), :]
        mixed = dot(zs[0][...], own[:, cols])
        for j in range(1, nt):
            mixed = mixed + dot(zs[j][...], wo[j - 1, :, cols])
        r = x + mixed
        resid[:, k * width : (k + 1) * width] = r
        sq = sq + jnp.sum(r * r, axis=1, keepdims=True)
    q2 = lax.rsqrt(sq / (nt * width) + EPS)
    q2_ref[...] = q2
    for k in range(nt):
        r = resid[:, k * width : (k + 1) * width]
        h2[:, k * width : (k + 1) * width] = (r * q2 * norm_two[pl.ds(t ^ k, 1), :]).astype(BF)
    big[0].wait()
    big[1].wait()
    hidden = gpre.shape[1]
    tile = tile_of(hidden)

    @pl.loop(0, hidden // tile)
    def _(i):
        cols = rows_at(i, tile)
        g = u = 0.0
        for k in range(nt):
            h = h2[:, k * width : (k + 1) * width]
            g = g + dot(h, wg[rows_at(t ^ k, width), cols])
            u = u + dot(h, wu[rows_at(t ^ k, width), cols])
        gpre[:, cols] = g
        upre[:, cols] = u
        act[:, cols] = (g * jax.nn.sigmoid(g) * u).astype(BF)


def backward_body(nt, groups, idx, *refs):
    refs = list(refs)

    def take(n):
        got, refs[:n] = refs[:n], []
        return got

    cs = take(nt)
    (norm_two,) = take(1)
    resid, q2_ref, gpre, upre = take(4)
    (own_hbm,) = take(1)
    held = take(len(groups))
    wg_hbm, wu_hbm, wd_hbm = take(3)
    dgate, dup, dz, mids = take(4)
    es = take(nt)
    zgs = take(nt - 1)
    own, wo, wg, wu, wd, sems, wsems = take(7)
    t, d = idx[0], idx[1]
    big = [pltpu.make_async_copy(a, b, wsems.at[i]) for i, (a, b) in enumerate(((wd_hbm, wd), (wg_hbm, wg), (wu_hbm, wu)))]
    for b in big:
        b.start()
    loads = start_mixer_weights(d, groups, held, own_hbm, own, wo, sems)
    width = cs[0].shape[1]
    hidden = gpre.shape[1]
    tile = tile_of(hidden)
    big[0].wait()

    def step(i, total):
        cols = rows_at(i, tile)
        dact = 0.0
        for k in range(nt):
            dact = dact + dot_t(cs[k][...], wd[cols, rows_at(t ^ k, width)])
        g = gpre[:, cols]
        u = upre[:, cols]
        sg = jax.nn.sigmoid(g)
        dg = (dact * u * sg * (1.0 + g * (1.0 - sg))).astype(BF)
        du = (dact * g * sg).astype(BF)
        dgate[:, cols] = dg
        dup[:, cols] = du
        return total + jnp.sum(dg.astype(F32) * g + du.astype(F32) * u, axis=1, keepdims=True)

    total = lax.fori_loop(0, hidden // tile, step, jnp.zeros((cs[0].shape[0], 1), F32))
    q2 = q2_ref[...]
    mean = total * q2 / (nt * width)
    big[1].wait()
    big[2].wait()
    for j in range(nt):
        rows = rows_at(t ^ j, width)
        dh = dot_t(dgate[...], wg[rows, :]) + dot_t(dup[...], wu[rows, :])
        n = resid[:, j * width : (j + 1) * width] * q2
        mids[j : j + 1, :] = jnp.sum(dh * n, axis=0, keepdims=True)
        es[j][...] = (q2 * (dh * norm_two[pl.ds(t ^ j, 1), :]) - n * mean).astype(BF)
    for load in loads:
        load.wait()
    for j in range(1, nt):
        zg = 0.0
        for k in range(nt):
            zg = zg + dot_t(es[k][...], wo[j - 1, :, rows_at(t ^ k, width)])
        zgs[j - 1][...] = zg.astype(BF)
    mine = 0.0
    for k in range(nt):
        part = own[:, rows_at(t ^ k, width)]
        mine = mine + dot_t(es[k][...], part) + dot_t(cs[k][...], part)
    dz[...] = mine


def split_rows(value):
    high = value.astype(BF)
    rest = value - high.astype(F32)
    mid = rest.astype(BF)
    return high, mid, (rest - mid.astype(F32)).astype(BF)


def hold_blocks(blocks, held, sem):
    width = held.shape[2]
    if len(blocks) == 1:
        blocks = [blocks[0].at[:, j * width : (j + 1) * width] for j in range(held.shape[0])]
    return [pltpu.make_async_copy(b, held.at[j], sem.at[j]) for j, b in enumerate(blocks)]


def turn_blocks(held, turned):
    width = held.shape[2]
    for j in range(held.shape[0]):
        turned[j * width : (j + 1) * width, :] = held[j].astype(F32).T.astype(BF)


def slot_product(held, turned, slot, step, b):
    if turned is not None:
        return dot(turned[rows_at(slot, step), :], b)
    sub = held.shape[2] // step
    cols = pl.ds(pl.multiple_of((slot % sub) * step, step), step)
    return lax.dot_general(held[slot // sub, :, cols], b, (((0,), (0,)), ((), ())), preferred_element_type=F32)


def mixer_back_body(nt, slots, step, idx, *refs):
    refs = list(refs)

    def take(n):
        got, refs[:n] = refs[:n], []
        return got

    (dz_ref,) = take(1)
    zgs = take(nt - 1)
    x_own, proj, conv, q1_ref, norm, mids, taps, r_own = take(8)
    xs = take(nt)
    w_hbm, wd_hbm, act = take(3)
    dproj, u_own, out_own, vec, first = take(5)
    us = take(nt - 1)
    w, wd, held, sem, xsem = take(5)
    turned = refs[0] if refs else None
    load = pltpu.make_async_copy(w_hbm, w, sem.at[0])
    load.start()
    down = pltpu.make_async_copy(wd_hbm, wd, sem.at[1])
    down.start()
    copies = hold_blocks(xs, held, xsem)
    for c in copies:
        c.start()
    t, by = idx[0], idx[2]
    rows, width = x_own.shape
    dz = dz_ref[...]
    for r in zgs:
        dz = dz + r[...].astype(F32)
    q1 = q1_ref[...]
    bgate = proj[:, :width]
    cgate = proj[:, width : 2 * width]
    xval = proj[:, 2 * width :]
    vmix = bgate * xval
    dcg = dz * conv[...]
    dconv = dz * cgate
    vec[...] = jnp.zeros(vec.shape, F32)
    vec[0:1, :] = jnp.sum(dconv * vmix, axis=0, keepdims=True)
    vec[1:2, :] = jnp.sum(dconv * back(vmix, 1), axis=0, keepdims=True)
    vec[2:3, :] = jnp.sum(dconv * back(vmix, 2), axis=0, keepdims=True)
    dv = taps[0:1, :] * dconv + taps[1:2, :] * fore(dconv, 1) + taps[2:3, :] * fore(dconv, 2)
    total = 0.0
    for at, value, saved in ((0, dv * xval, bgate), (1, dcg, cgate), (2, dv * bgate, xval)):
        value = (value * q1).astype(BF)
        dproj[:, at * width : (at + 1) * width] = value
        total = total + jnp.sum(value.astype(F32) * saved, axis=1, keepdims=True)
    mean = total * q1 / (nt * width)
    load.wait()
    for c in copies:
        c.wait()
    for j in range(nt):
        gain = norm[pl.ds(t ^ j, 1), :]
        x = x_own[...] if j == 0 else held[j].astype(F32) / gain
        dh = dot_t(dproj[...], w[rows_at(t ^ j, width), :])
        u = dh * gain - x * mean
        gain_sum = jnp.sum(dh * x, axis=0, keepdims=True)
        if j == 0:
            u_own[...] = u
            vec[3:4, :] = mids[0:1, :]
            vec[4:5, :] = gain_sum
        else:
            us[j - 1][0:rows, :] = u.astype(BF)
            zero = jnp.zeros((10, width), BF)
            us[j - 1][rows : rows + 16, :] = jnp.concatenate(
                [p.astype(F32) for p in split_rows(mids[j : j + 1, :]) + split_rows(gain_sum)]
                + [zero.astype(F32)],
                axis=0,
            ).astype(BF)
    if turned is not None:
        turn_blocks(held, turned)
    for at, e in enumerate(slots):
        first[at * step : (at + 1) * step, :] = slot_product(held, turned, e ^ by, step, dproj[...]).astype(BF)
    down.wait()
    out_own[...] = r_own[...] + dot(act[...], wd[:, rows_at(t, width)])
    for j in range(1, nt):
        us[j - 1][rows + 16 : 2 * rows + 16, :] = dot(act[...], wd[:, rows_at(t ^ j, width)]).astype(BF)


def finish_body(nt, dres, u_own, out_own, vec, *refs):
    got, (dx, out, small) = refs[: nt - 1], refs[nt - 1 :]
    rows = dx.shape[0]
    a, b, v = dres[...] + u_own[...], out_own[...], vec[...]
    place = lax.broadcasted_iota(jnp.int32, v.shape, 0)
    for r in got:
        a = a + r[0:rows, :].astype(F32)
        b = b + r[rows + 16 : 2 * rows + 16, :].astype(F32)
        s = r[rows : rows + 16, :].astype(F32)
        mid = s[0:1, :] + s[1:2, :] + s[2:3, :]
        gain = s[3:4, :] + s[4:5, :] + s[5:6, :]
        v = v + jnp.where(place == 3, mid, 0.0) + jnp.where(place == 4, gain, 0.0)
    dx[...] = a
    out[...] = b
    small[...] = v


def slot_plan(order):
    slots = [0]
    for b in reversed(order):
        slots = slots + [e | (1 << b) for e in slots]
    plan = []
    for _ in order:
        mid = len(slots) // 2
        plan.append((slots[mid:], slots[:mid]))
        slots = slots[:mid]
    return plan


def stage_body(plan, n_a, step, turn_out, idx, *refs):
    refs = list(refs)
    by = idx[2]
    a_refs = [refs.pop(0) for _ in range(n_a)]
    ins = []
    for slots, n_b, gots in plan:
        bs = [refs.pop(0) for _ in range(n_b)]
        ins.append((bs, [refs.pop(0) for _ in gots]))
    outs = [refs.pop(0) for _ in plan]
    held, asem = refs.pop(0), refs.pop(0)
    turned = refs.pop(0) if held.shape[2] // step and step % 128 else None
    copies = hold_blocks(a_refs, held, asem)
    for c in copies:
        c.start()
    work = []
    for (slots, n_b, gots), (bs, got) in zip(plan, ins):
        b_held, g_held, bsem, gsem = (refs.pop(0) for _ in range(4))
        start = 0
        for i, b in enumerate(bs):
            c = pltpu.make_async_copy(b, b_held.at[:, start : start + b.shape[1]], bsem.at[i])
            c.start()
            copies.append(c)
            start += b.shape[1]
        late = []
        for i, ((at_rows, col), g) in enumerate(zip(gots, got)):
            for p, row in enumerate(at_rows):
                src = g.at[row * step : (row + 1) * step, col : col + start]
                c = pltpu.make_async_copy(src, g_held.at[i, p], gsem.at[i, p])
                c.start()
                late.append(c)
        work.append((b_held, g_held, late))
    for c in copies:
        c.wait()
    if turned is not None:
        turn_blocks(held, turned)
    for (slots, n_b, gots), (b_held, g_held, late), out in zip(plan, work, outs):
        for c in late:
            c.wait()
        for p, e in enumerate(slots):
            value = slot_product(held, turned, e ^ by, step, b_held[...])
            for i in range(len(gots)):
                value = value + g_held[i, p].astype(F32)
            if turn_out:
                out[...] = value.T
            else:
                out[p * step : (p + 1) * step, :] = value.astype(out.dtype)


def stage(idx, a, streams, step, width, kind, turn_out=False):
    rows = a[0].shape[0]
    feats = width * len(a) if len(a) > 1 else a[0].shape[1]
    plan, args, outs, flops = [], [idx] + list(a), [], 0
    scratch = [pltpu.VMEM((feats // width, rows, width), BF), pltpu.SemaphoreType.DMA((feats // width,))]
    if step % 128:
        scratch.append(pltpu.VMEM((feats, rows), BF))
    for bs, slots, gots in streams:
        plan.append((tuple(slots), len(bs), tuple((tuple(has.index(e) for e in slots), col) for _, has, col in gots)))
        args.extend(bs)
        args.extend(g for g, _, _ in gots)
        cols = sum(b.shape[1] for b in bs)
        outs.append(shape((cols, step) if turn_out else (len(slots) * step, cols), kind))
        flops += 2 * rows * len(slots) * step * cols
        scratch += [
            pltpu.VMEM((rows, cols), BF),
            pltpu.VMEM((max(1, len(gots)), len(slots), step, cols), BF),
            pltpu.SemaphoreType.DMA((len(bs),)),
            pltpu.SemaphoreType.DMA((max(1, len(gots)), len(slots))),
        ]
    body = functools.partial(stage_body, tuple(plan), len(a), step, turn_out)
    return call(body, args, [SMEM] + [ANY] * (len(args) - 1), outs, scratch, flops, 24)


def mix_grad_body(plan, sub, step, turn_out, nt, idx, *refs):
    slots, n_in, gots = plan
    ins, zs = refs[:n_in], refs[n_in : n_in + nt]
    got = refs[n_in + nt : n_in + nt + len(gots)]
    outs = refs[n_in + nt + len(gots) : -5]
    turned, held, g_held, sem, gsem = refs[-5:]
    copies = hold_blocks(zs, held, sem)
    for i, (at_rows, g) in enumerate(zip(gots, got)):
        for p, row in enumerate(at_rows):
            copies.append(
                pltpu.make_async_copy(g.at[row * step : (row + 1) * step, :], g_held.at[i, p], gsem.at[i, p])
            )
    for c in copies:
        c.start()
    dres = ins[0][...]
    for r in ins[1:]:
        dres = dres + r[...].astype(F32)
    if n_in > 1:
        outs[1][...] = dres
    d = idx[1]
    turned[...] = dres.T.astype(BF)
    for c in copies:
        c.wait()
    for p, e in enumerate(slots):
        a = turned[rows_at((e % sub) ^ (d & (sub - 1)), step), :]
        value = dot(a, held[(e // sub) ^ (d // sub)])
        for i in range(len(gots)):
            value = value + g_held[i, p].astype(F32)
        if turn_out:
            outs[0][...] = value.T
        else:
            outs[0][p * step : (p + 1) * step, :] = value.astype(outs[0].dtype)


def per_device(nd, nt, block_in, norm_in, w_in, conv_w, w_out, norm_mid, w_gate, w_up, w_down, cot):
    t = lax.axis_index("tensor")
    d = lax.axis_index("dp")
    rows, width = block_in.shape[1:]
    feats = w_in.shape[0]
    hidden = w_gate.shape[1]
    sub = nd // nt
    step = feats // nd
    bits = list(range(nd.bit_length() - 1))
    order_one = bits
    order_two = bits[:1] + bits[2:3] + bits[1:2] + bits[3:]
    plan_one, plan_two = slot_plan(order_one), slot_plan(order_two)
    idx = jnp.stack([t, d, d ^ (sub * t)]).astype(jnp.int32)

    def over_tensor(arr, j):
        return lax.ppermute(arr, "tensor", [(i, i ^ j) for i in range(nt)])

    def over_dp(arr, e):
        return lax.ppermute(arr, "dp", [(i, i ^ e) for i in range(nd)])

    def gather(arr):
        return [over_tensor(arr, j) for j in range(1, nt)]

    def scatter(arrs):
        return [over_tensor(a, j + 1) for j, a in enumerate(arrs)]

    gain_one = norm_in.reshape(nt, width)
    gain_two = norm_mid.reshape(nt, width)
    x_own = block_in[0]
    gy_own = cot[0]
    x0 = (x_own * lax.dynamic_slice_in_dim(gain_one, t, 1, axis=0)).astype(BF)
    xs = gather(x0)
    w_flat = w_in.reshape(feats, 3 * width)

    share = width // nd
    part = lax.dynamic_slice_in_dim(w_out, d * share, share, axis=0)
    held = [jnp.stack(gather(part))[None]]
    groups = [[0]]
    held.append(over_dp(held[0], 1))
    groups.append([1])
    if nd == 8:
        pair = jnp.concatenate(held, axis=0)
        for e in (2, 4, 6):
            held.append(over_dp(pair, e))
            groups.append([e, e + 1])
    else:
        for b in bits[1:]:
            whole = jnp.concatenate(held, axis=0)
            held.append(over_dp(whole, 1 << b))
            groups.append([e | (1 << b) for e in range(1 << b)])
    groups = tuple(tuple(g) for g in groups)

    zmix, proj, conv, q1 = call(
        functools.partial(mixer_body, nt),
        [idx, x_own, x0] + xs + [gain_one, w_flat, conv_w],
        [SMEM] + [VMEM] * (2 + nt) + [ANY, VMEM],
        [shape((rows, width), BF), shape((rows, 3 * width), F32), shape((rows, width), F32), shape((rows, 1), F32)],
        [pltpu.VMEM((feats, 3 * width), BF), pltpu.SemaphoreType.DMA],
        2 * rows * w_flat.size,
    )
    zs = gather(zmix)
    c0 = gy_own.astype(BF)
    cs = [c0] + gather(c0)

    weights = [
        pltpu.VMEM((width, feats), BF),
        pltpu.VMEM((nt - 1, width, feats), BF),
        pltpu.VMEM((feats, hidden), BF),
        pltpu.VMEM((feats, hidden), BF),
        pltpu.VMEM((hidden, feats), BF),
        pltpu.SemaphoreType.DMA((1 + nd,)),
        pltpu.SemaphoreType.DMA((3,)),
    ]
    block = shape((rows, width), BF)
    blockf = shape((rows, width), F32)
    wide = shape((rows, hidden), F32)
    wideb = shape((rows, hidden), BF)
    resid, q2, h2, gpre, upre, act = call(
        functools.partial(forward_body, nt, groups),
        [idx, x_own] + xs + [gain_one, gain_two, zmix] + zs + [w_out] + held + [w_gate, w_up],
        [SMEM] + [VMEM] * (nt + 2 + nt) + [ANY] * (1 + len(held) + 2),
        [shape((rows, feats), F32), shape((rows, 1), F32), shape((rows, feats), BF), wide, wide, wideb],
        weights[:4] + weights[5:],
        2 * rows * (feats * feats + 2 * feats * hidden),
    )
    dgate, dup, dz, mids, *rest = call(
        functools.partial(backward_body, nt, groups),
        [idx] + cs + [gain_two, resid, q2, gpre, upre, w_out] + held + [w_gate, w_up, w_down],
        [SMEM] + [VMEM] * (nt + 5) + [ANY] * (1 + len(held) + 3),
        [wideb, wideb, blockf, shape((nt, width), F32)] + [block] * nt + [block] * (nt - 1),
        weights,
        2 * rows * (2 * feats * feats + 3 * feats * hidden),
    )
    es, zgs = rest[:nt], rest[nt:]
    zgs = scatter(zgs)
    e_got = scatter(es[1:])

    def sent(msg, e, slots):
        return over_dp(msg, e), [s ^ e for s in slots]

    down_got, gate_got, up_got = [], [], []
    for i, b in enumerate(order_two):
        slots = plan_two[i][0]
        (msg,) = stage(idx, cs, [([act], slots, down_got)], step, width, BF)
        down_got.append(sent(msg, 1 << b, slots) + (0,))
    turn_out = step % 128 == 0
    (s_down,) = stage(idx, cs, [([act], [0], down_got)], step, width, F32, turn_out)
    if not turn_out:
        s_down = s_down.T
    slots = plan_one[0][0]
    (msg,) = stage(idx, [h2], [([dgate, dup], slots, [])], step, width, BF)
    got = sent(msg, 1 << bits[0], slots)
    gate_got.append(got + (0,))
    up_got.append(got + (hidden,))
    for i in range(1, len(bits)):
        one, two = plan_one[i][0], plan_two[i][0]
        msg_one, msg_two = stage(idx, [h2], [([dgate], one, gate_got), ([dup], two, up_got)], step, width, BF)
        gate_got.append(sent(msg_one, 1 << order_one[i], one) + (0,))
        up_got.append(sent(msg_two, 1 << order_two[i], two) + (0,))
    s_gate, s_up = stage(idx, [h2], [([dgate], [0], gate_got), ([dup], [0], up_got)], step, width, F32)

    x_all = [x0] + xs
    slots = plan_two[0][0]
    extra = [pltpu.VMEM((feats, rows), BF)] if step % 128 else []
    message = shape((2 * rows + 16, width), BF)
    dproj, u_own, out_own, vec, first, *us = call(
        functools.partial(mixer_back_body, nt, tuple(slots), step),
        [idx, dz] + zgs + [x_own, proj, conv, q1, gain_one, mids, conv_w, resid[:, :width]]
        + x_all + [w_flat, w_down, act],
        [SMEM] + [VMEM] * (1 + (nt - 1) + 8) + [ANY] * nt + [ANY, ANY, VMEM],
        [shape((rows, 3 * width), BF), blockf, blockf, shape((8, width), F32), shape((len(slots) * step, 3 * width), BF)]
        + [message] * (nt - 1),
        [
            pltpu.VMEM((feats, 3 * width), BF),
            pltpu.VMEM((hidden, feats), BF),
            pltpu.VMEM((nt, rows, width), BF),
            pltpu.SemaphoreType.DMA((2,)),
            pltpu.SemaphoreType.DMA((nt,)),
        ] + extra,
        2 * rows * (2 * w_flat.size + w_down.size),
    )
    in_got = [sent(first, 1 << order_two[0], slots) + (0,)]
    us = scatter(us)
    for i in range(1, len(bits)):
        slots = plan_two[i][0]
        (msg,) = stage(idx, x_all, [([dproj], slots, in_got)], step, width, BF)
        in_got.append(sent(msg, 1 << order_two[i], slots) + (0,))
    (s_in,) = stage(idx, x_all, [([dproj], [0], in_got)], step, width, F32)

    z_all = [zmix] + zs

    def mix_grads(ins, slots, got, kind, last=False):
        plan = (tuple(slots), len(ins), tuple(tuple(has.index(e) for e in slots) for _, has in got))
        turns = last and turn_out
        outs = [shape((width, step) if turns else (len(slots) * step, width), kind)]
        if len(ins) > 1:
            outs.append(blockf)
        return call(
            functools.partial(mix_grad_body, plan, sub, step, turns, nt),
            [idx] + ins + z_all + [g for g, _ in got],
            [SMEM] + [VMEM] * len(ins) + [ANY] * (nt + len(got)),
            outs,
            [
                pltpu.VMEM((width, rows), BF),
                pltpu.VMEM((nt, rows, width), BF),
                pltpu.VMEM((max(1, len(got)), len(slots), step, width), BF),
                pltpu.SemaphoreType.DMA((nt,)),
                pltpu.SemaphoreType.DMA((max(1, len(got)), len(slots))),
            ],
            2 * rows * width * step * len(slots),
            16,
        )

    ins, out_got = [gy_own, es[0]] + e_got, []
    for i, b in enumerate(order_one):
        slots = plan_one[i][0]
        made = mix_grads(ins, slots, out_got, BF)
        if i == 0:
            dres = made[1]
            ins = [dres]
        out_got.append(sent(made[0], 1 << b, slots))
    (piece,) = mix_grads(ins, [0], out_got, F32, True)
    home = [
        (a * nt + b, (sub * b + a % sub) * nt + (b ^ (a // sub))) for a in range(nd) for b in range(nt)
    ]
    s_out = lax.ppermute(piece, ("dp", "tensor"), home)
    if not turn_out:
        s_out = s_out.T

    dx, out, small = call(
        functools.partial(finish_body, nt),
        [dres, u_own, out_own, vec] + us,
        [VMEM] * (4 + nt - 1),
        [blockf, blockf, shape((8, width), F32)],
        [],
        0,
        8,
    )
    for b in bits:
        small = small + over_dp(small, 1 << b)
    return (
        out[None],
        dx[None],
        small[4],
        s_in.reshape(step, 3, width),
        small[:3],
        s_out,
        small[3],
        s_gate,
        s_up,
        s_down,
    )


def solution(mesh):
    placed = (
        P("dp", None, "tensor"),
        P(),
        P(None, None, "tensor"),
        P(None, "tensor"),
        P("tensor", None),
        P(),
        P(None, "tensor"),
        P(None, "tensor"),
        P("tensor", None),
        P("dp", None, "tensor"),
    )

    def body(*args):
        return per_device(mesh.shape["dp"], mesh.shape["tensor"], *args)

    return jax.shard_map(
        body,
        mesh=mesh,
        in_specs=placed,
        out_specs=(
            P("dp", None, "tensor"),
            P("dp", None, "tensor"),
            P("tensor"),
            P("dp", None, "tensor"),
            P(None, "tensor"),
            P("tensor", "dp"),
            P("tensor"),
            P("dp", "tensor"),
            P("dp", "tensor"),
            P("tensor", "dp"),
        ),
        check_vma=False,
    )
```

```python
import functools

import jax
import jax.numpy as jnp
from jax import lax
from jax.experimental import pallas as pl
from jax.experimental.pallas import tpu as pltpu
from jax.sharding import PartitionSpec as P

EPS = 1e-05
BF = jnp.bfloat16
F32 = jnp.float32
ANY = pl.BlockSpec(memory_space=pl.ANY)
SMEM = pl.BlockSpec(memory_space=pltpu.SMEM)
VMEM = pl.BlockSpec(memory_space=pltpu.VMEM)


def dot(a, b):
    return jnp.dot(a, b, preferred_element_type=F32)


def dot_t(a, b):
    return lax.dot_general(a, b, (((1,), (1,)), ((), ())), preferred_element_type=F32)


def shape(dims, kind):
    return jax.ShapeDtypeStruct(tuple(dims), kind)


def call(body, args, specs, outs, scratch, flops, vmem=40):
    total = sum(a.size * a.dtype.itemsize for a in args) + sum(o.size * o.dtype.itemsize for o in outs)
    return pl.pallas_call(
        body,
        in_specs=specs,
        out_specs=[VMEM] * len(outs),
        out_shape=outs,
        scratch_shapes=scratch,
        cost_estimate=pl.CostEstimate(flops=int(flops), bytes_accessed=int(total), transcendentals=0),
        compiler_params=pltpu.CompilerParams(vmem_limit_bytes=vmem * 1024 * 1024),
    )(*args)


def rows_at(index, size):
    return pl.ds(pl.multiple_of(index * size, size), size)


def back(arr, k):
    place = lax.broadcasted_iota(jnp.int32, arr.shape, 0)
    return jnp.where(place >= k, pltpu.roll(arr, k, 0), 0.0)


def fore(arr, k):
    place = lax.broadcasted_iota(jnp.int32, arr.shape, 0)
    return jnp.where(place < arr.shape[0] - k, pltpu.roll(arr, arr.shape[0] - k, 0), 0.0)


def tile_of(size):
    for tile in (384, 256, 128):
        if size % tile == 0:
            return tile
    return size


def mixer_body(nt, idx, *refs):
    x_own = refs[0]
    xs = refs[1 : 1 + nt]
    norm, w, taps, zmix, proj, conv, q1_ref = refs[1 + nt :]
    t = idx[0]
    width = x_own.shape[1]
    x = x_own[...]
    sq = jnp.sum(x * x, axis=1, keepdims=True)
    for j in range(1, nt):
        v = xs[j][...].astype(F32) / norm[pl.ds(t ^ j, 1), :]
        sq = sq + jnp.sum(v * v, axis=1, keepdims=True)
    q1 = lax.rsqrt(sq / (nt * width) + EPS)
    q1_ref[...] = q1
    total = dot(xs[0][...], w[rows_at(t, width), :])
    for j in range(1, nt):
        total = total + dot(xs[j][...], w[rows_at(t ^ j, width), :])
    total = total * q1
    proj[...] = total
    bgate = total[:, :width]
    cgate = total[:, width : 2 * width]
    vmix = bgate * total[:, 2 * width :]
    cv = taps[0:1, :] * vmix + taps[1:2, :] * back(vmix, 1) + taps[2:3, :] * back(vmix, 2)
    conv[...] = cv
    zmix[...] = (cgate * cv).astype(BF)


def start_shares(d, groups, held, wo, sems):
    loads = []
    for ref, es in zip(held, groups):
        for at, e in enumerate(es):
            share = ref.shape[2]
            loads.append(pltpu.make_async_copy(ref.at[at], wo.at[:, rows_at(d ^ e, share), :], sems.at[e]))
    for load in loads:
        load.start()
    return loads


def forward_body(nt, groups, idx, *refs):
    refs = list(refs)

    def take(n):
        got, refs[:n] = refs[:n], []
        return got

    (x_own,) = take(1)
    xs = take(nt - 1)
    norm_one, norm_two = take(2)
    zs = take(nt)
    (own,) = take(1)
    held = take(len(groups))
    wg, wu = take(2)
    resid, q2_ref, h2, gpre, upre, act, wo, sems = take(8)
    t, d = idx[0], idx[1]
    loads = start_shares(d, groups, held, wo, sems)
    width = x_own.shape[1]
    for load in loads:
        load.wait()
    sq = 0.0
    for k in range(nt):
        cols = rows_at(t ^ k, width)
        x = x_own[...] if k == 0 else xs[k - 1][...].astype(F32) / norm_one[pl.ds(t ^ k, 1), :]
        mixed = dot(zs[0][...], own[:, cols])
        for j in range(1, nt):
            mixed = mixed + dot(zs[j][...], wo[j - 1, :, cols])
        r = x + mixed
        resid[:, k * width : (k + 1) * width] = r
        sq = sq + jnp.sum(r * r, axis=1, keepdims=True)
    q2 = lax.rsqrt(sq / (nt * width) + EPS)
    q2_ref[...] = q2
    for k in range(nt):
        r = resid[:, k * width : (k + 1) * width]
        h2[:, k * width : (k + 1) * width] = (r * q2 * norm_two[pl.ds(t ^ k, 1), :]).astype(BF)
    hidden = gpre.shape[1]
    tile = tile_of(hidden)

    @pl.loop(0, hidden // tile)
    def _(i):
        cols = rows_at(i, tile)
        g = u = 0.0
        for k in range(nt):
            h = h2[:, k * width : (k + 1) * width]
            g = g + dot(h, wg[rows_at(t ^ k, width), cols])
            u = u + dot(h, wu[rows_at(t ^ k, width), cols])
        gpre[:, cols] = g
        upre[:, cols] = u
        act[:, cols] = (g * jax.nn.sigmoid(g) * u).astype(BF)


def backward_body(nt, idx, *refs):
    refs = list(refs)

    def take(n):
        got, refs[:n] = refs[:n], []
        return got

    cs = take(nt)
    (norm_two,) = take(1)
    resid, q2_ref, gpre, upre = take(4)
    own, wo, wg, wu, wd = take(5)
    dgate, dup, dz, mids = take(4)
    es = take(nt)
    zgs = take(nt - 1)
    t = idx[0]
    width = cs[0].shape[1]
    hidden = gpre.shape[1]
    tile = tile_of(hidden)

    def step(i, total):
        cols = rows_at(i, tile)
        dact = 0.0
        for k in range(nt):
            dact = dact + dot_t(cs[k][...], wd[cols, rows_at(t ^ k, width)])
        g = gpre[:, cols]
        u = upre[:, cols]
        sg = jax.nn.sigmoid(g)
        dg = (dact * u * sg * (1.0 + g * (1.0 - sg))).astype(BF)
        du = (dact * g * sg).astype(BF)
        dgate[:, cols] = dg
        dup[:, cols] = du
        return total + jnp.sum(dg.astype(F32) * g + du.astype(F32) * u, axis=1, keepdims=True)

    total = lax.fori_loop(0, hidden // tile, step, jnp.zeros((cs[0].shape[0], 1), F32))
    q2 = q2_ref[...]
    mean = total * q2 / (nt * width)
    for j in range(nt):
        rows = rows_at(t ^ j, width)
        dh = dot_t(dgate[...], wg[rows, :]) + dot_t(dup[...], wu[rows, :])
        n = resid[:, j * width : (j + 1) * width] * q2
        mids[j : j + 1, :] = jnp.sum(dh * n, axis=0, keepdims=True)
        es[j][...] = (q2 * (dh * norm_two[pl.ds(t ^ j, 1), :]) - n * mean).astype(BF)
    for j in range(1, nt):
        zg = 0.0
        for k in range(nt):
            zg = zg + dot_t(es[k][...], wo[j - 1, :, rows_at(t ^ k, width)])
        zgs[j - 1][...] = zg.astype(BF)
    mine = 0.0
    for k in range(nt):
        part = own[:, rows_at(t ^ k, width)]
        mine = mine + dot_t(es[k][...], part) + dot_t(cs[k][...], part)
    dz[...] = mine


def split_rows(value):
    high = value.astype(BF)
    rest = value - high.astype(F32)
    mid = rest.astype(BF)
    return high, mid, (rest - mid.astype(F32)).astype(BF)


def hold_blocks(blocks, held, sem):
    width = held.shape[2]
    if len(blocks) == 1:
        blocks = [blocks[0].at[:, j * width : (j + 1) * width] for j in range(held.shape[0])]
    return [pltpu.make_async_copy(b, held.at[j], sem.at[j]) for j, b in enumerate(blocks)]


def turn_blocks(held, turned):
    width = held.shape[2]
    for j in range(held.shape[0]):
        turned[j * width : (j + 1) * width, :] = held[j].astype(F32).T.astype(BF)


def slot_product(held, turned, slot, step, b):
    if turned is not None:
        return dot(turned[rows_at(slot, step), :], b)
    sub = held.shape[2] // step
    cols = pl.ds(pl.multiple_of((slot % sub) * step, step), step)
    return lax.dot_general(held[slot // sub, :, cols], b, (((0,), (0,)), ((), ())), preferred_element_type=F32)


def mixer_back_body(nt, slots, step, idx, *refs):
    refs = list(refs)

    def take(n):
        got, refs[:n] = refs[:n], []
        return got

    (dz_ref,) = take(1)
    zgs = take(nt - 1)
    x_own, proj, conv, q1_ref, norm, mids, taps, r_own = take(8)
    xs = take(nt)
    w, wd, act = take(3)
    dproj, u_own, out_own, vec, first = take(5)
    us = take(nt - 1)
    held, xsem = take(2)
    turned = refs[0] if refs else None
    copies = hold_blocks(xs, held, xsem)
    for c in copies:
        c.start()
    t, by = idx[0], idx[2]
    rows, width = x_own.shape
    dz = dz_ref[...]
    for r in zgs:
        dz = dz + r[...].astype(F32)
    q1 = q1_ref[...]
    bgate = proj[:, :width]
    cgate = proj[:, width : 2 * width]
    xval = proj[:, 2 * width :]
    vmix = bgate * xval
    dcg = dz * conv[...]
    dconv = dz * cgate
    vec[...] = jnp.zeros(vec.shape, F32)
    vec[0:1, :] = jnp.sum(dconv * vmix, axis=0, keepdims=True)
    vec[1:2, :] = jnp.sum(dconv * back(vmix, 1), axis=0, keepdims=True)
    vec[2:3, :] = jnp.sum(dconv * back(vmix, 2), axis=0, keepdims=True)
    dv = taps[0:1, :] * dconv + taps[1:2, :] * fore(dconv, 1) + taps[2:3, :] * fore(dconv, 2)
    total = 0.0
    for at, value, saved in ((0, dv * xval, bgate), (1, dcg, cgate), (2, dv * bgate, xval)):
        value = (value * q1).astype(BF)
        dproj[:, at * width : (at + 1) * width] = value
        total = total + jnp.sum(value.astype(F32) * saved, axis=1, keepdims=True)
    mean = total * q1 / (nt * width)
    for c in copies:
        c.wait()
    for j in range(nt):
        gain = norm[pl.ds(t ^ j, 1), :]
        x = x_own[...] if j == 0 else held[j].astype(F32) / gain
        dh = dot_t(dproj[...], w[rows_at(t ^ j, width), :])
        u = dh * gain - x * mean
        gain_sum = jnp.sum(dh * x, axis=0, keepdims=True)
        if j == 0:
            u_own[...] = u
            vec[3:4, :] = mids[0:1, :]
            vec[4:5, :] = gain_sum
        else:
            us[j - 1][0:rows, :] = u.astype(BF)
            zero = jnp.zeros((10, width), BF)
            us[j - 1][rows : rows + 16, :] = jnp.concatenate(
                [p.astype(F32) for p in split_rows(mids[j : j + 1, :]) + split_rows(gain_sum)]
                + [zero.astype(F32)],
                axis=0,
            ).astype(BF)
    if turned is not None:
        turn_blocks(held, turned)
    for at, e in enumerate(slots):
        first[at * step : (at + 1) * step, :] = slot_product(held, turned, e ^ by, step, dproj[...]).astype(BF)
    out_own[...] = r_own[...] + dot(act[...], wd[:, rows_at(t, width)])
    for j in range(1, nt):
        us[j - 1][rows + 16 : 2 * rows + 16, :] = dot(act[...], wd[:, rows_at(t ^ j, width)]).astype(BF)


def finish_body(nt, dres, u_own, out_own, vec, *refs):
    got, (dx, out, small) = refs[: nt - 1], refs[nt - 1 :]
    rows = dx.shape[0]
    a, b, v = dres[...] + u_own[...], out_own[...], vec[...]
    place = lax.broadcasted_iota(jnp.int32, v.shape, 0)
    for r in got:
        a = a + r[0:rows, :].astype(F32)
        b = b + r[rows + 16 : 2 * rows + 16, :].astype(F32)
        s = r[rows : rows + 16, :].astype(F32)
        mid = s[0:1, :] + s[1:2, :] + s[2:3, :]
        gain = s[3:4, :] + s[4:5, :] + s[5:6, :]
        v = v + jnp.where(place == 3, mid, 0.0) + jnp.where(place == 4, gain, 0.0)
    dx[...] = a
    out[...] = b
    small[...] = v


def slot_plan(order):
    slots = [0]
    for b in reversed(order):
        slots = slots + [e | (1 << b) for e in slots]
    plan = []
    for _ in order:
        mid = len(slots) // 2
        plan.append((slots[mid:], slots[:mid]))
        slots = slots[:mid]
    return plan


def stage_body(plan, mix, n_z, n_a, sub, step, idx, *refs):
    refs = list(refs)
    d, by = idx[1], idx[2]
    a_refs = [[refs.pop(0) for _ in range(n)] for n in n_a]
    ins = [refs.pop(0) for _ in range(mix)]
    zs = [refs.pop(0) for _ in range(n_z)]
    n_b = 1 + max([b for parts, _, _, _ in plan for _, b, _, _ in parts])
    bs = [refs.pop(0) for _ in range(n_b)]
    gots = [[refs.pop(0) for _ in got] for _, _, got, _ in plan]
    n_out = 1 + max([o for _, _, _, outs in plan for _, o, _ in outs])
    outs = [refs.pop(0) for _ in range(n_out)]
    dres_out = refs.pop(0) if mix > 1 else None
    copies, held, turned = [], [], []
    for blocks in a_refs:
        h, sem = refs.pop(0), refs.pop(0)
        held.append(h)
        turned.append(refs.pop(0) if step % 128 else None)
        copies += hold_blocks(blocks, h, sem)
    if mix:
        dres_turned, z_held, z_sem = (refs.pop(0) for _ in range(3))
        copies += hold_blocks(zs, z_held, z_sem)
    work = []
    for (parts, slots, got, _), arrivals in zip(plan, gots):
        b_held, b_sem, g_held, g_sem = (refs.pop(0) for _ in range(4))
        start = 0
        for i, (a, b, lo, hi) in enumerate(parts):
            if a >= 0:
                copies.append(
                    pltpu.make_async_copy(bs[b].at[:, lo:hi], b_held.at[:, start : start + hi - lo], b_sem.at[i])
                )
            start += hi - lo
        for i, ((at_rows, first, last, col), g) in enumerate(zip(got, arrivals)):
            for p, row in enumerate(at_rows):
                src = g.at[row * step : (row + 1) * step, first:last]
                copies.append(pltpu.make_async_copy(src, g_held.at[i, p, :, col : col + last - first], g_sem.at[i, p]))
        work.append((b_held, g_held))
    for c in copies:
        c.start()
    if mix:
        dres = ins[0][...]
        for r in ins[1:]:
            dres = dres + r[...].astype(F32)
        if dres_out is not None:
            dres_out[...] = dres
        dres_turned[...] = dres.T.astype(BF)
    for c in copies:
        c.wait()
    for h, tu in zip(held, turned):
        if tu is not None:
            turn_blocks(h, tu)
    for (parts, slots, got, targets), (b_held, g_held) in zip(plan, work):
        for p, e in enumerate(slots):
            start = 0
            for (a, _, lo, hi), (form, o, place) in zip(parts, targets):
                cols = slice(start, start + hi - lo)
                if a < 0:
                    rows = dres_turned[rows_at((e % sub) ^ (d & (sub - 1)), step), :]
                    value = dot(rows, z_held[(e // sub) ^ (d // sub)])
                else:
                    value = slot_product(held[a], turned[a], e ^ by, step, b_held[:, cols])
                for i, (_, first, last, col) in enumerate(got):
                    if col <= start and start + hi - lo <= col + last - first:
                        value = value + g_held[i, p, :, cols].astype(F32)
                out = outs[o]
                if form == "turn":
                    out[place : place + hi - lo, :] = value.T
                elif form == "three":
                    for k in range(out.shape[1]):
                        out[:, k, :] = value[:, k * out.shape[2] : (k + 1) * out.shape[2]]
                else:
                    out[p * step : (p + 1) * step, place : place + hi - lo] = value.astype(out.dtype)
                start += hi - lo


def stage(idx, a_sets, mixed, bs, streams, outs, step, width, sub):
    rows = a_sets[0][0].shape[0] if a_sets else mixed[1][0].shape[0]
    args, scratch, plan, flops = [idx], [], [], 0
    specs = [SMEM]
    for blocks in a_sets:
        args += blocks
        n = sum(b.shape[1] for b in blocks) // width
        scratch += [pltpu.VMEM((n, rows, width), BF), pltpu.SemaphoreType.DMA((n,))]
        if step % 128:
            scratch.append(pltpu.VMEM((n * width, rows), BF))
    specs += [ANY] * (len(args) - 1)
    outs = list(outs)
    mix, n_z = 0, 0
    if mixed:
        ins, zs = mixed
        mix, n_z = len(ins), len(zs)
        args += ins + zs
        specs += [VMEM] * mix + [ANY] * len(zs)
        scratch += [
            pltpu.VMEM((width, rows), BF), pltpu.VMEM((len(zs), rows, width), BF), pltpu.SemaphoreType.DMA((len(zs),))
        ]
        if mix > 1:
            outs.append(shape((rows, width), F32))
    args += bs
    for parts, slots, got, targets in streams:
        args += [g[0] for g in got]
        cols = sum(hi - lo for _, _, lo, hi in parts)
        arrivals = tuple((tuple(has.index(e) for e in slots), first, last, col) for _, has, first, last, col in got)
        plan.append((tuple(parts), tuple(slots), arrivals, tuple(targets)))
        flops += 2 * rows * len(slots) * step * cols
        scratch += [
            pltpu.VMEM((rows, cols), BF),
            pltpu.SemaphoreType.DMA((len(parts),)),
            pltpu.VMEM((max(1, len(got)), len(slots), step, cols), BF),
            pltpu.SemaphoreType.DMA((max(1, len(got)), len(slots))),
        ]
    specs += [ANY] * (len(args) - len(specs))
    body = functools.partial(stage_body, tuple(plan), mix, n_z, tuple(len(a) for a in a_sets), sub, step)
    return call(body, args, specs, outs, scratch, flops, 24)


def last_body(small, more, conv, mid, norm):
    total = small[...] + more[...]
    conv[...] = total[0:3, :]
    mid[...] = total[3:4, :]
    norm[...] = total[4:5, :]


def per_device(nd, nt, block_in, norm_in, w_in, conv_w, w_out, norm_mid, w_gate, w_up, w_down, cot):
    t = lax.axis_index("tensor")
    d = lax.axis_index("dp")
    rows, width = block_in.shape[1:]
    feats = w_in.shape[0]
    hidden = w_gate.shape[1]
    sub = nd // nt
    step = feats // nd
    bits = list(range(nd.bit_length() - 1))
    order_one = bits
    order_two = bits[:1] + bits[2:3] + bits[1:2] + bits[3:]
    plan_one, plan_two = slot_plan(order_one), slot_plan(order_two)
    idx = jnp.stack([t, d, d ^ (sub * t)]).astype(jnp.int32)

    def over_tensor(arr, j):
        return lax.ppermute(arr, "tensor", [(i, i ^ j) for i in range(nt)])

    def over_dp(arr, e):
        return lax.ppermute(arr, "dp", [(i, i ^ e) for i in range(nd)])

    def gather(arr):
        return [over_tensor(arr, j) for j in range(1, nt)]

    def scatter(arrs):
        return [over_tensor(a, j + 1) for j, a in enumerate(arrs)]

    gain_one = norm_in.reshape(nt, width)
    gain_two = norm_mid.reshape(nt, width)
    x_own = block_in[0]
    gy_own = cot[0]
    x0 = (x_own * lax.dynamic_slice_in_dim(gain_one, t, 1, axis=0)).astype(BF)
    xs = gather(x0)
    w_flat = w_in.reshape(feats, 3 * width)

    share = width // nd
    part = lax.dynamic_slice_in_dim(w_out, d * share, share, axis=0)
    held = [jnp.stack(gather(part))[None]]
    groups = [[0]]
    if nd == 8:
        for e in (2, 4, 6):
            held.append(over_dp(held[0], e))
            groups.append([e])
        for e in (0, 2, 4, 6):
            held.append(over_dp(held[e // 2], 1))
            groups.append([e + 1])
    else:
        for b in bits:
            whole = jnp.concatenate(held, axis=0)
            held.append(over_dp(whole, 1 << b))
            groups.append([e | (1 << b) for e in range(1 << b)])
    groups = tuple(tuple(g) for g in groups)

    zmix, proj, conv, q1 = call(
        functools.partial(mixer_body, nt),
        [idx, x_own, x0] + xs + [gain_one, w_flat, conv_w],
        [SMEM] + [VMEM] * (2 + nt) + [VMEM, VMEM],
        [shape((rows, width), BF), shape((rows, 3 * width), F32), shape((rows, width), F32), shape((rows, 1), F32)],
        [],
        2 * rows * w_flat.size,
        12,
    )
    zs = gather(zmix)
    c0 = gy_own.astype(BF)
    cs = [c0] + gather(c0)

    block = shape((rows, width), BF)
    blockf = shape((rows, width), F32)
    wide = shape((rows, hidden), F32)
    wideb = shape((rows, hidden), BF)
    resid, q2, h2, gpre, upre, act, wo = call(
        functools.partial(forward_body, nt, groups),
        [idx, x_own] + xs + [gain_one, gain_two, zmix] + zs + [w_out] + held + [w_gate, w_up],
        [SMEM] + [VMEM] * (nt + 2 + nt + 1) + [ANY] * len(held) + [VMEM] * 2,
        [shape((rows, feats), F32), shape((rows, 1), F32), shape((rows, feats), BF), wide, wide, wideb]
        + [shape((nt - 1, width, feats), BF)],
        [pltpu.SemaphoreType.DMA((nd,))],
        2 * rows * (feats * feats + 2 * feats * hidden),
        24,
    )
    dgate, dup, dz, mids, *rest = call(
        functools.partial(backward_body, nt),
        [idx] + cs + [gain_two, resid, q2, gpre, upre, w_out, wo, w_gate, w_up, w_down],
        [SMEM] + [VMEM] * (nt + 10),
        [wideb, wideb, blockf, shape((nt, width), F32)] + [block] * nt + [block] * (nt - 1),
        [],
        2 * rows * (2 * feats * feats + 3 * feats * hidden),
        24,
    )
    es, zgs = rest[:nt], rest[nt:]
    zgs = scatter(zgs)
    e_got = scatter(es[1:])

    def sent(msg, e, slots):
        return over_dp(msg, e), [s ^ e for s in slots]

    def run(a_sets, mixed, bs, streams, outs):
        return stage(idx, a_sets, mixed, bs, streams, outs, step, width, sub)

    cut = (hidden // 128 + 1) // 2 * 128 if hidden % 128 == 0 else hidden
    bs = [dgate, dup, act]
    one = [(0, 0, 0, hidden), (1, 2, 0, cut)]
    two = [(0, 1, 0, hidden), (1, 2, cut, hidden)]
    total_one, total_two = hidden + cut, 2 * hidden - cut
    flat_one = [("flat", 0, 0), ("flat", 0, hidden)]
    flat_two = [("flat", 1, 0), ("flat", 1, hidden)]
    slots = plan_one[0][0]
    (msg,) = run(
        [[h2], cs], None, bs,
        [(one + two, slots, [], flat_one + [("flat", 0, total_one), ("flat", 0, total_one + hidden)])],
        [shape((len(slots) * step, total_one + total_two), BF)],
    )
    got = sent(msg, 1 << bits[0], slots)
    got_one = [got + (0, total_one, 0)]
    got_two = [got + (total_one, total_one + total_two, 0)]
    for i in range(1, len(bits)):
        s_one, s_two = plan_one[i][0], plan_two[i][0]
        m_one, m_two = run(
            [[h2], cs], None, bs, [(one, s_one, got_one, flat_one), (two, s_two, got_two, flat_two)],
            [shape((len(s_one) * step, total_one), BF), shape((len(s_two) * step, total_two), BF)],
        )
        got_one.append(sent(m_one, 1 << order_one[i], s_one) + (0, total_one, 0))
        got_two.append(sent(m_two, 1 << order_two[i], s_two) + (0, total_two, 0))
    turns = step % 128 == 0
    down = shape((hidden, step) if turns else (step, hidden), F32)
    form = "turn" if turns else "flat"
    s_gate, s_up, s_down = run(
        [[h2], cs], None, bs,
        [
            (one, [0], got_one, [("flat", 0, 0), (form, 2, 0)]),
            (two, [0], got_two, [("flat", 1, 0), (form, 2, cut)]),
        ],
        [shape((step, hidden), F32), shape((step, hidden), F32), down],
    )
    if not turns:
        s_down = s_down.T

    x_all = [x0] + xs
    slots = plan_two[0][0]
    extra = [pltpu.VMEM((feats, rows), BF)] if step % 128 else []
    message = shape((2 * rows + 16, width), BF)
    dproj, u_own, out_own, vec, first, *us = call(
        functools.partial(mixer_back_body, nt, tuple(slots), step),
        [idx, dz] + zgs + [x_own, proj, conv, q1, gain_one, mids, conv_w, resid[:, :width]]
        + x_all + [w_flat, w_down, act],
        [SMEM] + [VMEM] * (1 + (nt - 1) + 8) + [ANY] * nt + [VMEM] * 3,
        [shape((rows, 3 * width), BF), blockf, blockf, shape((8, width), F32), shape((len(slots) * step, 3 * width), BF)]
        + [message] * (nt - 1),
        [pltpu.VMEM((nt, rows, width), BF), pltpu.SemaphoreType.DMA((nt,))] + extra,
        2 * rows * (2 * w_flat.size + w_down.size),
        24,
    )
    cols = 3 * width
    io_got = [sent(first, 1 << order_two[0], slots) + (0, cols, 0)]
    us = scatter(us)

    z_all = [zmix] + zs
    ins = [gy_own, es[0]] + e_got
    msg, dres = run(
        [], (ins, z_all), [gy_own], [([(-1, 0, 0, width)], slots, [], [("flat", 0, 0)])],
        [shape((len(slots) * step, width), BF)],
    )
    io_got.append(sent(msg, 1 << order_two[0], slots) + (0, width, cols))
    both = [(0, 0, 0, cols), (-1, 0, 0, width)]
    for i in range(1, len(bits)):
        slots = plan_two[i][0]
        (msg,) = run(
            [x_all], ([dres], z_all), [dproj], [(both, slots, io_got, [("flat", 0, 0), ("flat", 0, cols)])],
            [shape((len(slots) * step, cols + width), BF)],
        )
        io_got.append(sent(msg, 1 << order_two[i], slots) + (0, cols + width, 0))
    s_in, piece = run(
        [x_all], ([dres], z_all), [dproj], [(both, [0], io_got, [("three", 0, 0), (form, 1, 0)])],
        [shape((step, 3, width), F32), shape((width, step) if turns else (step, width), F32)],
    )
    home = [
        (a * nt + b, (sub * b + a % sub) * nt + (b ^ (a // sub))) for a in range(nd) for b in range(nt)
    ]
    s_out = lax.ppermute(piece, ("dp", "tensor"), home)
    if not turns:
        s_out = s_out.T

    dx, out, small = call(
        functools.partial(finish_body, nt),
        [dres, u_own, out_own, vec] + us,
        [VMEM] * (4 + nt - 1),
        [blockf, blockf, shape((8, width), F32)],
        [],
        0,
        8,
    )
    for b in bits:
        more = over_dp(small, 1 << b)
        if b != bits[-1]:
            small = small + more
    row = shape((1, width), F32)
    s_conv, s_mid, s_norm = call(last_body, [small, more], [VMEM] * 2, [shape((3, width), F32), row, row], [], 0, 8)
    return (
        out[None],
        dx[None],
        s_norm[0],
        s_in,
        s_conv,
        s_out,
        s_mid[0],
        s_gate,
        s_up,
        s_down,
    )


def solution(mesh):
    placed = (
        P("dp", None, "tensor"),
        P(),
        P(None, None, "tensor"),
        P(None, "tensor"),
        P("tensor", None),
        P(),
        P(None, "tensor"),
        P(None, "tensor"),
        P("tensor", None),
        P("dp", None, "tensor"),
    )

    def body(*args):
        return per_device(mesh.shape["dp"], mesh.shape["tensor"], *args)

    return jax.shard_map(
        body,
        mesh=mesh,
        in_specs=placed,
        out_specs=(
            P("dp", None, "tensor"),
            P("dp", None, "tensor"),
            P("tensor"),
            P("dp", None, "tensor"),
            P(None, "tensor"),
            P("tensor", "dp"),
            P("tensor"),
            P("dp", "tensor"),
            P("dp", "tensor"),
            P("tensor", "dp"),
        ),
        check_vma=False,
    )
```

```python
import functools

import jax
import jax.numpy as jnp
from jax import lax
from jax.experimental import pallas as pl
from jax.experimental.pallas import tpu as pltpu
from jax.sharding import PartitionSpec as P

EPS = 1e-05
BF = jnp.bfloat16
F32 = jnp.float32
ANY = pl.BlockSpec(memory_space=pl.ANY)
SMEM = pl.BlockSpec(memory_space=pltpu.SMEM)
VMEM = pl.BlockSpec(memory_space=pltpu.VMEM)


def dot(a, b):
    return jnp.dot(a, b, preferred_element_type=F32)


def dot_t(a, b):
    return lax.dot_general(a, b, (((1,), (1,)), ((), ())), preferred_element_type=F32)


def shape(dims, kind):
    return jax.ShapeDtypeStruct(tuple(dims), kind)


def call(body, args, specs, outs, scratch, flops, vmem=40):
    total = sum(a.size * a.dtype.itemsize for a in args) + sum(o.size * o.dtype.itemsize for o in outs)
    return pl.pallas_call(
        body,
        in_specs=specs,
        out_specs=[VMEM] * len(outs),
        out_shape=outs,
        scratch_shapes=scratch,
        cost_estimate=pl.CostEstimate(flops=int(flops), bytes_accessed=int(total), transcendentals=0),
        compiler_params=pltpu.CompilerParams(vmem_limit_bytes=vmem * 1024 * 1024),
    )(*args)


def rows_at(index, size):
    return pl.ds(pl.multiple_of(index * size, size), size)


def back(arr, k):
    place = lax.broadcasted_iota(jnp.int32, arr.shape, 0)
    return jnp.where(place >= k, pltpu.roll(arr, k, 0), 0.0)


def fore(arr, k):
    place = lax.broadcasted_iota(jnp.int32, arr.shape, 0)
    return jnp.where(place < arr.shape[0] - k, pltpu.roll(arr, arr.shape[0] - k, 0), 0.0)


def tile_of(size):
    for tile in (384, 256, 128):
        if size % tile == 0:
            return tile
    return size


def load_body(n, *refs):
    src, dst, sem = refs[:n], refs[n : 2 * n], refs[2 * n]
    copies = [pltpu.make_async_copy(a, b, sem.at[i]) for i, (a, b) in enumerate(zip(src, dst))]
    for c in copies:
        c.start()
    for c in copies:
        c.wait()


def mixer_body(nt, idx, *refs):
    x_own = refs[0]
    xs = refs[1 : 1 + nt]
    norm, w, taps, zmix, proj, conv, q1_ref = refs[1 + nt :]
    t = idx[0]
    width = x_own.shape[1]
    x = x_own[...]
    sq = jnp.sum(x * x, axis=1, keepdims=True)
    for j in range(1, nt):
        v = xs[j][...].astype(F32) / norm[pl.ds(t ^ j, 1), :]
        sq = sq + jnp.sum(v * v, axis=1, keepdims=True)
    q1 = lax.rsqrt(sq / (nt * width) + EPS)
    q1_ref[...] = q1
    parts = []
    for k in range(3):
        total = dot(xs[0][...], w[k, rows_at(t, width), :])
        for j in range(1, nt):
            total = total + dot(xs[j][...], w[k, rows_at(t ^ j, width), :])
        parts.append(total * q1)
        proj[:, k * width : (k + 1) * width] = parts[k]
    cgate = parts[1]
    vmix = parts[0] * parts[2]
    cv = taps[0:1, :] * vmix + taps[1:2, :] * back(vmix, 1) + taps[2:3, :] * back(vmix, 2)
    conv[...] = cv
    zmix[...] = (cgate * cv).astype(BF)


def start_shares(d, groups, held, wo, sems):
    loads = []
    for ref, es in zip(held, groups):
        for at, e in enumerate(es):
            share = ref.shape[2]
            loads.append(pltpu.make_async_copy(ref.at[at], wo.at[:, rows_at(d ^ e, share), :], sems.at[e]))
    for load in loads:
        load.start()
    return loads


def forward_body(nt, groups, idx, *refs):
    refs = list(refs)

    def take(n):
        got, refs[:n] = refs[:n], []
        return got

    (x_own,) = take(1)
    xs = take(nt - 1)
    norm_one, norm_two = take(2)
    zs = take(nt)
    (own,) = take(1)
    held = take(len(groups))
    wg, wu = take(2)
    resid, q2_ref, h2, gpre, upre, act, wo, sems = take(8)
    t, d = idx[0], idx[1]
    loads = start_shares(d, groups, held, wo, sems)
    width = x_own.shape[1]
    for load in loads:
        load.wait()
    sq = 0.0
    for k in range(nt):
        cols = rows_at(t ^ k, width)
        x = x_own[...] if k == 0 else xs[k - 1][...].astype(F32) / norm_one[pl.ds(t ^ k, 1), :]
        mixed = dot(zs[0][...], own[:, cols])
        for j in range(1, nt):
            mixed = mixed + dot(zs[j][...], wo[j - 1, :, cols])
        r = x + mixed
        resid[:, k * width : (k + 1) * width] = r
        sq = sq + jnp.sum(r * r, axis=1, keepdims=True)
    q2 = lax.rsqrt(sq / (nt * width) + EPS)
    q2_ref[...] = q2
    for k in range(nt):
        r = resid[:, k * width : (k + 1) * width]
        h2[:, k * width : (k + 1) * width] = (r * q2 * norm_two[pl.ds(t ^ k, 1), :]).astype(BF)
    hidden = gpre.shape[1]
    tile = tile_of(hidden)

    @pl.loop(0, hidden // tile)
    def _(i):
        cols = rows_at(i, tile)
        g = u = 0.0
        for k in range(nt):
            h = h2[:, k * width : (k + 1) * width]
            g = g + dot(h, wg[rows_at(t ^ k, width), cols])
            u = u + dot(h, wu[rows_at(t ^ k, width), cols])
        gpre[:, cols] = g
        upre[:, cols] = u
        act[:, cols] = (g * jax.nn.sigmoid(g) * u).astype(BF)


def backward_body(nt, idx, *refs):
    refs = list(refs)

    def take(n):
        got, refs[:n] = refs[:n], []
        return got

    cs = take(nt)
    (norm_two,) = take(1)
    resid, q2_ref, gpre, upre = take(4)
    own, wo, wg, wu, wd = take(5)
    dgate, dup, dz, mids = take(4)
    es = take(nt)
    zgs = take(nt - 1)
    t = idx[0]
    width = cs[0].shape[1]
    hidden = gpre.shape[1]
    tile = tile_of(hidden)

    def step(i, total):
        cols = rows_at(i, tile)
        dact = 0.0
        for k in range(nt):
            dact = dact + dot_t(cs[k][...], wd[cols, rows_at(t ^ k, width)])
        g = gpre[:, cols]
        u = upre[:, cols]
        sg = jax.nn.sigmoid(g)
        dg = (dact * u * sg * (1.0 + g * (1.0 - sg))).astype(BF)
        du = (dact * g * sg).astype(BF)
        dgate[:, cols] = dg
        dup[:, cols] = du
        return total + jnp.sum(dg.astype(F32) * g + du.astype(F32) * u, axis=1, keepdims=True)

    total = lax.fori_loop(0, hidden // tile, step, jnp.zeros((cs[0].shape[0], 1), F32))
    q2 = q2_ref[...]
    mean = total * q2 / (nt * width)
    for j in range(nt):
        rows = rows_at(t ^ j, width)
        dh = dot_t(dgate[...], wg[rows, :]) + dot_t(dup[...], wu[rows, :])
        n = resid[:, j * width : (j + 1) * width] * q2
        mids[j : j + 1, :] = jnp.sum(dh * n, axis=0, keepdims=True)
        es[j][...] = (q2 * (dh * norm_two[pl.ds(t ^ j, 1), :]) - n * mean).astype(BF)
    for j in range(1, nt):
        zg = 0.0
        for k in range(nt):
            zg = zg + dot_t(es[k][...], wo[j - 1, :, rows_at(t ^ k, width)])
        zgs[j - 1][...] = zg.astype(BF)
    mine = 0.0
    for k in range(nt):
        part = own[:, rows_at(t ^ k, width)]
        mine = mine + dot_t(es[k][...], part) + dot_t(cs[k][...], part)
    dz[...] = mine


def split_rows(value):
    high = value.astype(BF)
    rest = value - high.astype(F32)
    mid = rest.astype(BF)
    return high, mid, (rest - mid.astype(F32)).astype(BF)


def hold_blocks(blocks, held, sem):
    width = held.shape[2]
    if len(blocks) == 1:
        blocks = [blocks[0].at[:, j * width : (j + 1) * width] for j in range(held.shape[0])]
    return [pltpu.make_async_copy(b, held.at[j], sem.at[j]) for j, b in enumerate(blocks)]


def turn_blocks(held, turned):
    width = held.shape[2]
    for j in range(held.shape[0]):
        turned[j * width : (j + 1) * width, :] = held[j].astype(F32).T.astype(BF)


def slot_product(held, turned, slot, step, b):
    if turned is not None:
        return dot(turned[rows_at(slot, step), :], b)
    sub = held.shape[2] // step
    cols = pl.ds(pl.multiple_of((slot % sub) * step, step), step)
    return lax.dot_general(held[slot // sub, :, cols], b, (((0,), (0,)), ((), ())), preferred_element_type=F32)


def mixer_back_body(nt, slots, step, idx, *refs):
    refs = list(refs)

    def take(n):
        got, refs[:n] = refs[:n], []
        return got

    (dz_ref,) = take(1)
    zgs = take(nt - 1)
    x_own, proj, conv, q1_ref, norm, mids, taps, r_own = take(8)
    xs = take(nt)
    w, wd, act = take(3)
    dproj, u_own, out_own, vec, first = take(5)
    us = take(nt - 1)
    held, xsem = take(2)
    turned = refs[0] if refs else None
    copies = hold_blocks(xs, held, xsem)
    for c in copies:
        c.start()
    t, by = idx[0], idx[2]
    rows, width = x_own.shape
    dz = dz_ref[...]
    for r in zgs:
        dz = dz + r[...].astype(F32)
    q1 = q1_ref[...]
    bgate = proj[:, :width]
    cgate = proj[:, width : 2 * width]
    xval = proj[:, 2 * width :]
    vmix = bgate * xval
    dcg = dz * conv[...]
    dconv = dz * cgate
    vec[...] = jnp.zeros(vec.shape, F32)
    vec[0:1, :] = jnp.sum(dconv * vmix, axis=0, keepdims=True)
    vec[1:2, :] = jnp.sum(dconv * back(vmix, 1), axis=0, keepdims=True)
    vec[2:3, :] = jnp.sum(dconv * back(vmix, 2), axis=0, keepdims=True)
    dv = taps[0:1, :] * dconv + taps[1:2, :] * fore(dconv, 1) + taps[2:3, :] * fore(dconv, 2)
    total = 0.0
    for at, value, saved in ((0, dv * xval, bgate), (1, dcg, cgate), (2, dv * bgate, xval)):
        value = (value * q1).astype(BF)
        dproj[:, at * width : (at + 1) * width] = value
        total = total + jnp.sum(value.astype(F32) * saved, axis=1, keepdims=True)
    mean = total * q1 / (nt * width)
    for c in copies:
        c.wait()
    for j in range(nt):
        gain = norm[pl.ds(t ^ j, 1), :]
        x = x_own[...] if j == 0 else held[j].astype(F32) / gain
        dh = 0.0
        for k in range(3):
            dh = dh + dot_t(dproj[:, k * width : (k + 1) * width], w[k, rows_at(t ^ j, width), :])
        u = dh * gain - x * mean
        gain_sum = jnp.sum(dh * x, axis=0, keepdims=True)
        if j == 0:
            u_own[...] = u
            vec[3:4, :] = mids[0:1, :]
            vec[4:5, :] = gain_sum
        else:
            us[j - 1][0:rows, :] = u.astype(BF)
            zero = jnp.zeros((10, width), BF)
            us[j - 1][rows : rows + 16, :] = jnp.concatenate(
                [p.astype(F32) for p in split_rows(mids[j : j + 1, :]) + split_rows(gain_sum)]
                + [zero.astype(F32)],
                axis=0,
            ).astype(BF)
    if turned is not None:
        turn_blocks(held, turned)
    for at, e in enumerate(slots):
        first[at * step : (at + 1) * step, :] = slot_product(held, turned, e ^ by, step, dproj[...]).astype(BF)
    out_own[...] = r_own[...] + dot(act[...], wd[:, rows_at(t, width)])
    for j in range(1, nt):
        us[j - 1][rows + 16 : 2 * rows + 16, :] = dot(act[...], wd[:, rows_at(t ^ j, width)]).astype(BF)


def finish_body(nt, dres, u_own, out_own, vec, *refs):
    got, (dx, out, small) = refs[: nt - 1], refs[nt - 1 :]
    rows = dx.shape[0]
    a, b, v = dres[...] + u_own[...], out_own[...], vec[...]
    place = lax.broadcasted_iota(jnp.int32, v.shape, 0)
    for r in got:
        a = a + r[0:rows, :].astype(F32)
        b = b + r[rows + 16 : 2 * rows + 16, :].astype(F32)
        s = r[rows : rows + 16, :].astype(F32)
        mid = s[0:1, :] + s[1:2, :] + s[2:3, :]
        gain = s[3:4, :] + s[4:5, :] + s[5:6, :]
        v = v + jnp.where(place == 3, mid, 0.0) + jnp.where(place == 4, gain, 0.0)
    dx[...] = a
    out[...] = b
    small[...] = v


def slot_plan(order):
    slots = [0]
    for b in reversed(order):
        slots = slots + [e | (1 << b) for e in slots]
    plan = []
    for _ in order:
        mid = len(slots) // 2
        plan.append((slots[mid:], slots[:mid]))
        slots = slots[:mid]
    return plan


def stage_body(plan, mix, n_z, n_a, sub, step, idx, *refs):
    refs = list(refs)
    d, by = idx[1], idx[2]
    a_refs = [[refs.pop(0) for _ in range(n)] for n in n_a]
    ins = [refs.pop(0) for _ in range(mix)]
    zs = [refs.pop(0) for _ in range(n_z)]
    n_b = 1 + max([b for parts, _, _, _ in plan for _, b, _, _ in parts])
    bs = [refs.pop(0) for _ in range(n_b)]
    gots = [[refs.pop(0) for _ in got] for _, _, got, _ in plan]
    n_out = 1 + max([o for _, _, _, outs in plan for _, o, _ in outs])
    outs = [refs.pop(0) for _ in range(n_out)]
    dres_out = refs.pop(0) if mix > 1 else None
    copies, held, turned = [], [], []
    for blocks in a_refs:
        h, sem = refs.pop(0), refs.pop(0)
        held.append(h)
        turned.append(refs.pop(0) if step % 128 else None)
        copies += hold_blocks(blocks, h, sem)
    if mix:
        dres_turned, z_held, z_sem = (refs.pop(0) for _ in range(3))
        copies += hold_blocks(zs, z_held, z_sem)
    work = []
    for (parts, slots, got, _), arrivals in zip(plan, gots):
        b_held, b_sem, g_held, g_sem = (refs.pop(0) for _ in range(4))
        start = 0
        for i, (a, b, lo, hi) in enumerate(parts):
            if a >= 0:
                copies.append(
                    pltpu.make_async_copy(bs[b].at[:, lo:hi], b_held.at[:, start : start + hi - lo], b_sem.at[i])
                )
            start += hi - lo
        for i, ((at_rows, first, last, col), g) in enumerate(zip(got, arrivals)):
            for p, row in enumerate(at_rows):
                src = g.at[row * step : (row + 1) * step, first:last]
                copies.append(pltpu.make_async_copy(src, g_held.at[i, p, :, col : col + last - first], g_sem.at[i, p]))
        work.append((b_held, g_held))
    for c in copies:
        c.start()
    if mix:
        dres = ins[0][...]
        for r in ins[1:]:
            dres = dres + r[...].astype(F32)
        if dres_out is not None:
            dres_out[...] = dres
        dres_turned[...] = dres.T.astype(BF)
    for c in copies:
        c.wait()
    for h, tu in zip(held, turned):
        if tu is not None:
            turn_blocks(h, tu)
    for (parts, slots, got, targets), (b_held, g_held) in zip(plan, work):
        for p, e in enumerate(slots):
            start = 0
            for (a, _, lo, hi), (form, o, place) in zip(parts, targets):
                cols = slice(start, start + hi - lo)
                if form is not None and form != e:
                    start += hi - lo
                    continue
                if a < 0:
                    rows = dres_turned[rows_at((e % sub) ^ (d & (sub - 1)), step), :]
                    value = dot(rows, z_held[(e // sub) ^ (d // sub)])
                else:
                    value = slot_product(held[a], turned[a], e ^ by, step, b_held[:, cols])
                for i, (_, first, last, col) in enumerate(got):
                    if col <= start and start + hi - lo <= col + last - first:
                        value = value + g_held[i, p, :, cols].astype(F32)
                out = outs[o]
                if form is not None:
                    out[:, place : place + hi - lo] = value.astype(out.dtype)
                else:
                    out[p * step : (p + 1) * step, place : place + hi - lo] = value.astype(out.dtype)
                start += hi - lo


def stage(idx, a_sets, mixed, bs, streams, outs, step, width, sub):
    rows = a_sets[0][0].shape[0] if a_sets else mixed[1][0].shape[0]
    args, scratch, plan, flops = [idx], [], [], 0
    specs = [SMEM]
    for blocks in a_sets:
        args += blocks
        n = sum(b.shape[1] for b in blocks) // width
        scratch += [pltpu.VMEM((n, rows, width), BF), pltpu.SemaphoreType.DMA((n,))]
        if step % 128:
            scratch.append(pltpu.VMEM((n * width, rows), BF))
    specs += [ANY] * (len(args) - 1)
    outs = list(outs)
    mix, n_z = 0, 0
    if mixed:
        ins, zs = mixed
        mix, n_z = len(ins), len(zs)
        args += ins + zs
        specs += [VMEM] * mix + [ANY] * len(zs)
        scratch += [
            pltpu.VMEM((width, rows), BF), pltpu.VMEM((len(zs), rows, width), BF), pltpu.SemaphoreType.DMA((len(zs),))
        ]
        if mix > 1:
            outs.append(shape((rows, width), F32))
    args += bs
    for parts, slots, got, targets in streams:
        args += [g[0] for g in got]
        cols = sum(hi - lo for _, _, lo, hi in parts)
        arrivals = tuple((tuple(has.index(e) for e in slots), first, last, col) for _, has, first, last, col in got)
        plan.append((tuple(parts), tuple(slots), arrivals, tuple(targets)))
        flops += 2 * rows * len(slots) * step * cols
        scratch += [
            pltpu.VMEM((rows, cols), BF),
            pltpu.SemaphoreType.DMA((len(parts),)),
            pltpu.VMEM((max(1, len(got)), len(slots), step, cols), BF),
            pltpu.SemaphoreType.DMA((max(1, len(got)), len(slots))),
        ]
    specs += [ANY] * (len(args) - len(specs))
    body = functools.partial(stage_body, tuple(plan), mix, n_z, tuple(len(a) for a in a_sets), sub, step)
    return call(body, args, specs, outs, scratch, flops, 24)


def ffn_end_body(cut, turns, one, two, got_one, got_two, gate, up, down):
    hidden = gate.shape[1]
    gate[...] = one[:, :hidden] + got_one[:, :hidden].astype(F32)
    up[...] = two[:, :hidden] + got_two[:, :hidden].astype(F32)
    low = one[:, hidden:] + got_one[:, hidden:].astype(F32)
    if turns:
        down[:cut, :] = low.T
    else:
        down[:, :cut] = low
    if cut < hidden:
        high = two[:, hidden:] + got_two[:, hidden:].astype(F32)
        if turns:
            down[cut:, :] = high.T
        else:
            down[:, cut:] = high


def io_end_body(cut, one, two, got_one, got_two, out):
    width = out.shape[2]
    low = one[...] + got_one[...].astype(F32)
    high = two[...] + got_two[...].astype(F32)
    for k in range(3):
        at = k * width
        out[k] = low[:, at : at + width] if at < cut else high[:, at - cut : at - cut + width]


def last_body(turns, small, more, piece_one, piece_two, conv, mid, norm, out):
    total = small[...] + more[...]
    conv[...] = total[0:3, :]
    mid[...] = total[3:4, :]
    norm[...] = total[4:5, :]
    piece = piece_one[...].astype(F32) + piece_two[...].astype(F32)
    out[...] = piece.T if turns else piece


def per_device(nd, nt, block_in, norm_in, w_in, conv_w, w_out, norm_mid, w_gate, w_up, w_down, cot):
    t = lax.axis_index("tensor")
    d = lax.axis_index("dp")
    rows, width = block_in.shape[1:]
    feats = w_in.shape[0]
    hidden = w_gate.shape[1]
    sub = nd // nt
    step = feats // nd
    bits = list(range(nd.bit_length() - 1))
    order_one = bits
    order_two = bits[:1] + bits[2:3] + bits[1:2] + bits[3:]
    plan_one, plan_two = slot_plan(order_one), slot_plan(order_two)
    idx = jnp.stack([t, d, d ^ (sub * t)]).astype(jnp.int32)

    def over_tensor(arr, j):
        return lax.ppermute(arr, "tensor", [(i, i ^ j) for i in range(nt)])

    def over_dp(arr, e):
        return lax.ppermute(arr, "dp", [(i, i ^ e) for i in range(nd)])

    def gather(arr):
        return [over_tensor(arr, j) for j in range(1, nt)]

    def scatter(arrs):
        return [over_tensor(a, j + 1) for j, a in enumerate(arrs)]

    gain_one = norm_in.reshape(nt, width)
    gain_two = norm_mid.reshape(nt, width)
    x_own = block_in[0]
    gy_own = cot[0]
    x0 = (x_own * lax.dynamic_slice_in_dim(norm_in, t * width, width)[None]).astype(BF)
    xs = gather(x0)
    w_three = jnp.transpose(w_in, (1, 0, 2))
    raw = [w_three, w_gate, w_up, w_down, w_out]
    w_three, w_gate, w_up, w_down, w_own = call(
        functools.partial(load_body, len(raw)),
        raw, [ANY] * len(raw), [shape(a.shape, a.dtype) for a in raw], [pltpu.SemaphoreType.DMA((len(raw),))], 0, 1,
    )

    share = width // nd
    part = lax.dynamic_slice_in_dim(w_out, d * share, share, axis=0)
    shares = gather(part)
    held = [jnp.stack(shares)[None]]
    groups = [[0]]
    if nd == 8:
        for e in (2, 4, 6):
            held.append(over_dp(held[0], e))
            groups.append([e])
        for e in (0, 2, 4, 6):
            held.append(over_dp(held[e // 2], 1))
            groups.append([e + 1])
    else:
        for b in bits:
            whole = jnp.concatenate(held, axis=0)
            held.append(over_dp(whole, 1 << b))
            groups.append([e | (1 << b) for e in range(1 << b)])
    groups = tuple(tuple(g) for g in groups)

    zmix, proj, conv, q1 = call(
        functools.partial(mixer_body, nt),
        [idx, x_own, x0] + xs + [gain_one, w_three, conv_w],
        [SMEM] + [VMEM] * (2 + nt) + [VMEM, VMEM],
        [shape((rows, width), BF), shape((rows, 3 * width), F32), shape((rows, width), F32), shape((rows, 1), F32)],
        [],
        2 * rows * w_in.size,
        8,
    )
    zs = gather(zmix)
    c0 = gy_own.astype(BF)
    cs = [c0] + gather(c0)

    block = shape((rows, width), BF)
    blockf = shape((rows, width), F32)
    wide = shape((rows, hidden), F32)
    wideb = shape((rows, hidden), BF)
    resid, q2, h2, gpre, upre, act, wo = call(
        functools.partial(forward_body, nt, groups),
        [idx, x_own] + xs + [gain_one, gain_two, zmix] + zs + [w_own] + held + [w_gate, w_up],
        [SMEM] + [VMEM] * (nt + 2 + nt + 1) + [ANY] * len(held) + [VMEM] * 2,
        [shape((rows, feats), F32), shape((rows, 1), F32), shape((rows, feats), BF), wide, wide, wideb]
        + [shape((nt - 1, width, feats), BF)],
        [pltpu.SemaphoreType.DMA((nd,))],
        2 * rows * (feats * feats + 2 * feats * hidden),
        24,
    )
    dgate, dup, dz, mids, *rest = call(
        functools.partial(backward_body, nt),
        [idx] + cs + [gain_two, resid, q2, gpre, upre, w_own, wo, w_gate, w_up, w_down],
        [SMEM] + [VMEM] * (nt + 10),
        [wideb, wideb, blockf, shape((nt, width), F32)] + [block] * nt + [block] * (nt - 1),
        [],
        2 * rows * (2 * feats * feats + 3 * feats * hidden),
        24,
    )
    es, zgs = rest[:nt], rest[nt:]
    zgs = scatter(zgs)
    e_got = scatter(es[1:])

    def sent(msg, e, slots):
        return over_dp(msg, e), [s ^ e for s in slots]

    def run(a_sets, mixed, bs, streams, outs):
        return stage(idx, a_sets, mixed, bs, streams, outs, step, width, sub)

    cut = (hidden // 128 + 1) // 2 * 128 if hidden % 128 == 0 else hidden
    bs = [dgate, dup, act]
    one = [(0, 0, 0, hidden), (1, 2, 0, cut)]
    two = [(0, 1, 0, hidden), (1, 2, cut, hidden)]
    total_one, total_two = hidden + cut, 2 * hidden - cut
    flat_one = [(None, 0, 0), (None, 0, hidden)]
    flat_two = [(None, 1, 0), (None, 1, hidden)]
    keep_one = [(0, 2, 0), (0, 2, hidden)]
    keep_two = [(0, 3, 0), (0, 3, hidden)]
    slots = plan_one[0][0]
    (msg,) = run(
        [[h2], cs], None, bs,
        [(one + two, slots, [], flat_one + [(None, 0, total_one), (None, 0, total_one + hidden)])],
        [shape((len(slots) * step, total_one + total_two), BF)],
    )
    got = sent(msg, 1 << bits[0], slots)
    got_one = [got + (0, total_one, 0)]
    got_two = [got + (total_one, total_one + total_two, 0)]
    for i in range(1, len(bits)):
        s_one, s_two = plan_one[i][0], plan_two[i][0]
        streams = [(one, s_one, got_one, flat_one), (two, s_two, got_two, flat_two)]
        outs = [shape((len(s_one) * step, total_one), BF), shape((len(s_two) * step, total_two), BF)]
        if i == len(bits) - 1:
            streams += [(one, [0], got_one, keep_one), (two, [0], got_two, keep_two)]
            outs += [shape((step, total_one), F32), shape((step, total_two), F32)]
        m_one, m_two, *kept = run([[h2], cs], None, bs, streams, outs)
        last_one = sent(m_one, 1 << order_one[i], s_one)
        last_two = sent(m_two, 1 << order_two[i], s_two)
        got_one = got_one + [last_one + (0, total_one, 0)]
        got_two = got_two + [last_two + (0, total_two, 0)]
    turns = step % 128 == 0
    down = shape((hidden, step) if turns else (step, hidden), F32)
    s_gate, s_up, s_down = call(
        functools.partial(ffn_end_body, cut, turns),
        kept + [last_one[0], last_two[0]], [VMEM] * 4, [shape((step, hidden), F32)] * 2 + [down], [], 0, 12,
    )
    if not turns:
        s_down = s_down.T

    x_all = [x0] + xs
    slots = plan_two[0][0]
    extra = [pltpu.VMEM((feats, rows), BF)] if step % 128 else []
    message = shape((2 * rows + 16, width), BF)
    dproj, u_own, out_own, vec, first, *us = call(
        functools.partial(mixer_back_body, nt, tuple(slots), step),
        [idx, dz] + zgs + [x_own, proj, conv, q1, gain_one, mids, conv_w, resid[:, :width]]
        + x_all + [w_three, w_down, act],
        [SMEM] + [VMEM] * (1 + (nt - 1) + 8) + [ANY] * nt + [VMEM] * 3,
        [shape((rows, 3 * width), BF), blockf, blockf, shape((8, width), F32), shape((len(slots) * step, 3 * width), BF)]
        + [message] * (nt - 1),
        [pltpu.VMEM((nt, rows, width), BF), pltpu.SemaphoreType.DMA((nt,))] + extra,
        2 * rows * (2 * w_in.size + w_down.size),
        24,
    )
    cols = 3 * width
    split = 2 * width
    sin = sent(first, 1 << order_two[0], slots)
    us = scatter(us)

    z_all = [zmix] + zs
    ins = [gy_own, es[0]] + e_got
    msg, dres = run(
        [], (ins, z_all), [gy_own], [([(-1, 0, 0, width)], slots, [], [(None, 0, 0)])],
        [shape((len(slots) * step, width), BF)],
    )
    smix = sent(msg, 1 << order_two[0], slots)
    high = cols - split
    got_one = [sin + (0, split, 0)]
    got_two = [sin + (split, cols, 0), smix + (0, width, high)]
    one = [(0, 0, 0, split)]
    two = [(0, 0, split, cols), (-1, 0, 0, width)]
    for i in range(1, len(bits)):
        s_one, s_two = plan_one[i][0], plan_two[i][0]
        if i < len(bits) - 1:
            m_one, m_two = run(
                [x_all], ([dres], z_all), [dproj],
                [(one, s_one, got_one, [(None, 0, 0)]), (two, s_two, got_two, [(None, 1, 0), (None, 1, high)])],
                [shape((len(s_one) * step, split), BF), shape((len(s_two) * step, high + width), BF)],
            )
        else:
            piece = shape((step, width), BF)
            m_one, m_two, kept_one, kept_two, far, near = run(
                [x_all], ([dres], z_all), [dproj],
                [
                    (one, s_one, got_one, [(None, 0, 0)]),
                    (two, s_two, got_two, [(None, 1, 0), (None, 4, 0)]),
                    (one, [0], got_one, [(0, 2, 0)]),
                    (two, [0], got_two, [(0, 3, 0), (None, 5, 0)]),
                ],
                [
                    shape((step, split), BF), shape((step, high), BF), shape((step, split), F32), shape((step, high), F32),
                    piece, piece,
                ],
            )
        end_one = sent(m_one, 1 << order_one[i], s_one)
        end_two = sent(m_two, 1 << order_two[i], s_two)
        got_one = got_one + [end_one + (0, split, 0)]
        got_two = got_two + [end_two + (0, high + width, 0)]
    s_in = call(
        functools.partial(io_end_body, split),
        [kept_one, kept_two, end_one[0], end_two[0]], [VMEM] * 4, [shape((3, step, width), F32)], [], 0, 8,
    )[0]
    s_in = jnp.transpose(s_in, (1, 0, 2))

    def home(piece, e):
        return lax.ppermute(
            piece, ("dp", "tensor"),
            [
                (a * nt + b, (sub * b + (a ^ e) % sub) * nt + (b ^ ((a ^ e) // sub)))
                for a in range(nd) for b in range(nt)
            ],
        )

    pieces = [home(far, 1 << order_two[-1]), home(near, 0)]

    dx, out, small = call(
        functools.partial(finish_body, nt),
        [dres, u_own, out_own, vec] + us,
        [VMEM] * (4 + nt - 1),
        [blockf, blockf, shape((8, width), F32)],
        [],
        0,
        8,
    )
    for b in bits:
        more = over_dp(small, 1 << b)
        if b != bits[-1]:
            small = small + more
    row = shape((1, width), F32)
    s_conv, s_mid, s_norm, s_out = call(
        functools.partial(last_body, turns), [small, more] + pieces, [VMEM] * 4,
        [shape((3, width), F32), row, row, shape((width, step) if turns else (step, width), F32)], [], 0, 8,
    )
    if not turns:
        s_out = s_out.T
    return (
        out[None],
        dx[None],
        s_norm[0],
        s_in,
        s_conv,
        s_out,
        s_mid[0],
        s_gate,
        s_up,
        s_down,
    )


def solution(mesh):
    placed = (
        P("dp", None, "tensor"),
        P(),
        P(None, None, "tensor"),
        P(None, "tensor"),
        P("tensor", None),
        P(),
        P(None, "tensor"),
        P(None, "tensor"),
        P("tensor", None),
        P("dp", None, "tensor"),
    )

    def body(*args):
        return per_device(mesh.shape["dp"], mesh.shape["tensor"], *args)

    return jax.shard_map(
        body,
        mesh=mesh,
        in_specs=placed,
        out_specs=(
            P("dp", None, "tensor"),
            P("dp", None, "tensor"),
            P("tensor"),
            P("dp", None, "tensor"),
            P(None, "tensor"),
            P("tensor", "dp"),
            P("tensor"),
            P("dp", "tensor"),
            P("dp", "tensor"),
            P("tensor", "dp"),
        ),
        check_vma=False,
    )
```

```python
import functools

import jax
import jax.numpy as jnp
from jax import lax
from jax.experimental import pallas as pl
from jax.experimental.pallas import tpu as pltpu
from jax.sharding import PartitionSpec as P

EPS = 1e-05
BF = jnp.bfloat16
F32 = jnp.float32
ANY = pl.BlockSpec(memory_space=pl.ANY)
SMEM = pl.BlockSpec(memory_space=pltpu.SMEM)
VMEM = pl.BlockSpec(memory_space=pltpu.VMEM)


def dot(a, b):
    return jnp.dot(a, b, preferred_element_type=F32)


def dot_t(a, b):
    return lax.dot_general(a, b, (((1,), (1,)), ((), ())), preferred_element_type=F32)


def shape(dims, kind):
    return jax.ShapeDtypeStruct(tuple(dims), kind)


def call(body, args, specs, outs, scratch, flops, vmem=40):
    total = sum(a.size * a.dtype.itemsize for a in args) + sum(o.size * o.dtype.itemsize for o in outs)
    return pl.pallas_call(
        body,
        in_specs=specs,
        out_specs=[VMEM] * len(outs),
        out_shape=outs,
        scratch_shapes=scratch,
        cost_estimate=pl.CostEstimate(flops=int(flops), bytes_accessed=int(total), transcendentals=0),
        compiler_params=pltpu.CompilerParams(vmem_limit_bytes=vmem * 1024 * 1024),
    )(*args)


def rows_at(index, size):
    return pl.ds(pl.multiple_of(index * size, size), size)


def back(arr, k):
    place = lax.broadcasted_iota(jnp.int32, arr.shape, 0)
    return jnp.where(place >= k, pltpu.roll(arr, k, 0), 0.0)


def fore(arr, k):
    place = lax.broadcasted_iota(jnp.int32, arr.shape, 0)
    return jnp.where(place < arr.shape[0] - k, pltpu.roll(arr, arr.shape[0] - k, 0), 0.0)


def tile_of(size):
    for tile in (384, 256, 128):
        if size % tile == 0:
            return tile
    return size


def mixer_body(nt, idx, *refs):
    x_own = refs[0]
    xs = refs[1 : 1 + nt]
    norm, w, taps, zmix, proj, conv, q1_ref = refs[1 + nt :]
    t = idx[0]
    width = x_own.shape[1]
    x = x_own[...]
    sq = jnp.sum(x * x, axis=1, keepdims=True)
    for j in range(1, nt):
        v = xs[j][...].astype(F32) / norm[pl.ds(t ^ j, 1), :]
        sq = sq + jnp.sum(v * v, axis=1, keepdims=True)
    q1 = lax.rsqrt(sq / (nt * width) + EPS)
    q1_ref[...] = q1
    parts = []
    for k in range(3):
        total = dot(xs[0][...], w[k, rows_at(t, width), :])
        for j in range(1, nt):
            total = total + dot(xs[j][...], w[k, rows_at(t ^ j, width), :])
        parts.append(total * q1)
        proj[:, k * width : (k + 1) * width] = parts[k]
    cgate = parts[1]
    vmix = parts[0] * parts[2]
    cv = taps[0:1, :] * vmix + taps[1:2, :] * back(vmix, 1) + taps[2:3, :] * back(vmix, 2)
    conv[...] = cv
    zmix[...] = (cgate * cv).astype(BF)


def start_shares(d, groups, held, wo, sems):
    loads = []
    for ref, es in zip(held, groups):
        for at, e in enumerate(es):
            share = ref.shape[2]
            loads.append(pltpu.make_async_copy(ref.at[at], wo.at[:, rows_at(d ^ e, share), :], sems.at[e]))
    for load in loads:
        load.start()
    return loads


def forward_body(nt, groups, idx, *refs):
    refs = list(refs)

    def take(n):
        got, refs[:n] = refs[:n], []
        return got

    (x_own,) = take(1)
    xs = take(nt - 1)
    (gains,) = take(1)
    zs = take(nt)
    (own,) = take(1)
    held = take(len(groups))
    wg, wu = take(2)
    resid, q2_ref, h2, gpre, upre, act, wo, sems = take(8)
    t, d = idx[0], idx[1]
    loads = start_shares(d, groups, held, wo, sems)
    width = x_own.shape[1]
    for load in loads:
        load.wait()
    sq = 0.0
    for k in range(nt):
        cols = rows_at(t ^ k, width)
        x = x_own[...] if k == 0 else xs[k - 1][...].astype(F32) / gains[pl.ds(t ^ k, 1), :]
        mixed = dot(zs[0][...], own[:, cols])
        for j in range(1, nt):
            mixed = mixed + dot(zs[j][...], wo[j - 1, :, cols])
        r = x + mixed
        resid[:, k * width : (k + 1) * width] = r
        sq = sq + jnp.sum(r * r, axis=1, keepdims=True)
    q2 = lax.rsqrt(sq / (nt * width) + EPS)
    q2_ref[...] = q2
    for k in range(nt):
        r = resid[:, k * width : (k + 1) * width]
        h2[:, k * width : (k + 1) * width] = (r * q2 * gains[pl.ds(nt + (t ^ k), 1), :]).astype(BF)
    hidden = gpre.shape[1]
    tile = tile_of(hidden)

    @pl.loop(0, hidden // tile)
    def _(i):
        cols = rows_at(i, tile)
        g = u = 0.0
        for k in range(nt):
            h = h2[:, k * width : (k + 1) * width]
            g = g + dot(h, wg[rows_at(t ^ k, width), cols])
            u = u + dot(h, wu[rows_at(t ^ k, width), cols])
        gpre[:, cols] = g
        upre[:, cols] = u
        act[:, cols] = (g * jax.nn.sigmoid(g) * u).astype(BF)


def backward_body(nt, idx, *refs):
    refs = list(refs)

    def take(n):
        got, refs[:n] = refs[:n], []
        return got

    cs = take(nt)
    (norm_two,) = take(1)
    resid, q2_ref, gpre, upre = take(4)
    own, wo, wg, wu, wd = take(5)
    dgate, dup, dz, mids = take(4)
    es = take(nt)
    zgs = take(nt - 1)
    t = idx[0]
    width = cs[0].shape[1]
    hidden = gpre.shape[1]
    tile = tile_of(hidden)

    def step(i, total):
        cols = rows_at(i, tile)
        dact = 0.0
        for k in range(nt):
            dact = dact + dot_t(cs[k][...], wd[cols, rows_at(t ^ k, width)])
        g = gpre[:, cols]
        u = upre[:, cols]
        sg = jax.nn.sigmoid(g)
        dg = (dact * u * sg * (1.0 + g * (1.0 - sg))).astype(BF)
        du = (dact * g * sg).astype(BF)
        dgate[:, cols] = dg
        dup[:, cols] = du
        return total + jnp.sum(dg.astype(F32) * g + du.astype(F32) * u, axis=1, keepdims=True)

    total = lax.fori_loop(0, hidden // tile, step, jnp.zeros((cs[0].shape[0], 1), F32))
    q2 = q2_ref[...]
    mean = total * q2 / (nt * width)
    for j in range(nt):
        rows = rows_at(t ^ j, width)
        dh = dot_t(dgate[...], wg[rows, :]) + dot_t(dup[...], wu[rows, :])
        n = resid[:, j * width : (j + 1) * width] * q2
        mids[j : j + 1, :] = jnp.sum(dh * n, axis=0, keepdims=True)
        es[j][...] = (q2 * (dh * norm_two[pl.ds(nt + (t ^ j), 1), :]) - n * mean).astype(BF)
    for j in range(1, nt):
        zg = 0.0
        for k in range(nt):
            zg = zg + dot_t(es[k][...], wo[j - 1, :, rows_at(t ^ k, width)])
        zgs[j - 1][...] = zg.astype(BF)
    mine = 0.0
    for k in range(nt):
        part = own[:, rows_at(t ^ k, width)]
        mine = mine + dot_t(es[k][...], part) + dot_t(cs[k][...], part)
    dz[...] = mine


def hold_blocks(blocks, held, sem):
    width = held.shape[2]
    if len(blocks) == 1:
        blocks = [blocks[0].at[:, j * width : (j + 1) * width] for j in range(held.shape[0])]
    return [pltpu.make_async_copy(b, held.at[j], sem.at[j]) for j, b in enumerate(blocks)]


def turn_blocks(held, turned):
    width = held.shape[2]
    for j in range(held.shape[0]):
        turned[j * width : (j + 1) * width, :] = held[j].astype(F32).T.astype(BF)


def slot_product(held, turned, slot, step, b):
    if turned is not None:
        return dot(turned[rows_at(slot, step), :], b)
    sub = held.shape[2] // step
    cols = pl.ds(pl.multiple_of((slot % sub) * step, step), step)
    return lax.dot_general(held[slot // sub, :, cols], b, (((0,), (0,)), ((), ())), preferred_element_type=F32)


def mixer_back_body(nt, slots, step, idx, *refs):
    refs = list(refs)

    def take(n):
        got, refs[:n] = refs[:n], []
        return got

    (dz_ref,) = take(1)
    zgs = take(nt - 1)
    x_own, proj, conv, q1_ref, norm, mids, taps, r_own = take(8)
    xs = take(nt)
    w, wd, act = take(3)
    dproj, u_own, out_own, vec, first = take(5)
    us = take(nt - 1)
    held, xsem = take(2)
    turned = refs[0] if refs else None
    copies = hold_blocks(xs, held, xsem)
    for c in copies:
        c.start()
    t, by = idx[0], idx[2]
    rows, width = x_own.shape
    dz = dz_ref[...]
    for r in zgs:
        dz = dz + r[...].astype(F32)
    q1 = q1_ref[...]
    bgate = proj[:, :width]
    cgate = proj[:, width : 2 * width]
    xval = proj[:, 2 * width :]
    vmix = bgate * xval
    dcg = dz * conv[...]
    dconv = dz * cgate
    vec[...] = jnp.zeros(vec.shape, F32)
    vec[0:1, :] = jnp.sum(dconv * vmix, axis=0, keepdims=True)
    vec[1:2, :] = jnp.sum(dconv * back(vmix, 1), axis=0, keepdims=True)
    vec[2:3, :] = jnp.sum(dconv * back(vmix, 2), axis=0, keepdims=True)
    dv = taps[0:1, :] * dconv + taps[1:2, :] * fore(dconv, 1) + taps[2:3, :] * fore(dconv, 2)
    total = 0.0
    for at, value, saved in ((0, dv * xval, bgate), (1, dcg, cgate), (2, dv * bgate, xval)):
        value = (value * q1).astype(BF)
        dproj[:, at * width : (at + 1) * width] = value
        total = total + jnp.sum(value.astype(F32) * saved, axis=1, keepdims=True)
    mean = total * q1 / (nt * width)
    for c in copies:
        c.wait()
    for j in range(nt):
        gain = norm[pl.ds(t ^ j, 1), :]
        x = x_own[...] if j == 0 else held[j].astype(F32) / gain
        dh = 0.0
        for k in range(3):
            dh = dh + dot_t(dproj[:, k * width : (k + 1) * width], w[k, rows_at(t ^ j, width), :])
        u = dh * gain - x * mean
        gain_sum = jnp.sum(dh * x, axis=0, keepdims=True)
        vec[4 + j : 5 + j, :] = mids[j : j + 1, :]
        vec[4 + nt + j : 5 + nt + j, :] = gain_sum
        if j == 0:
            u_own[...] = u
        else:
            us[j - 1][0:rows, :] = u.astype(BF)
    if turned is not None:
        turn_blocks(held, turned)
    for at, e in enumerate(slots):
        first[at * step : (at + 1) * step, :] = slot_product(held, turned, e ^ by, step, dproj[...]).astype(BF)
    out_own[...] = r_own[...] + dot(act[...], wd[:, rows_at(t, width)])
    for j in range(1, nt):
        us[j - 1][rows : 2 * rows, :] = dot(act[...], wd[:, rows_at(t ^ j, width)]).astype(BF)


def finish_body(nt, dres, u_own, out_own, *refs):
    got, (dx, out) = refs[: nt - 1], refs[nt - 1 :]
    rows = dx.shape[0]
    a, b = dres[...] + u_own[...], out_own[...]
    for r in got:
        a = a + r[0:rows, :].astype(F32)
        b = b + r[rows : 2 * rows, :].astype(F32)
    dx[...] = a
    out[...] = b


def slot_plan(order):
    slots = [0]
    for b in reversed(order):
        slots = slots + [e | (1 << b) for e in slots]
    plan = []
    for _ in order:
        mid = len(slots) // 2
        plan.append((slots[mid:], slots[:mid]))
        slots = slots[:mid]
    return plan


def stage_body(plan, mix, n_z, n_a, sub, step, idx, *refs):
    refs = list(refs)
    d, by = idx[1], idx[2]
    a_refs = [[refs.pop(0) for _ in range(n)] for n in n_a]
    ins = [refs.pop(0) for _ in range(mix)]
    zs = [refs.pop(0) for _ in range(n_z)]
    n_b = 1 + max([b for parts, _, _, _ in plan for _, b, _, _ in parts])
    bs = [refs.pop(0) for _ in range(n_b)]
    gots = [[refs.pop(0) for _ in got] for _, _, got, _ in plan]
    n_out = 1 + max([o for _, _, _, outs in plan for _, o, _ in outs])
    outs = [refs.pop(0) for _ in range(n_out)]
    dres_out = refs.pop(0) if mix > 1 else None
    copies, held, turned = [], [], []
    for blocks in a_refs:
        h, sem = refs.pop(0), refs.pop(0)
        held.append(h)
        turned.append(refs.pop(0) if step % 128 else None)
        copies += hold_blocks(blocks, h, sem)
    if mix:
        dres_turned, z_held, z_sem = (refs.pop(0) for _ in range(3))
        copies += hold_blocks(zs, z_held, z_sem)
    work = []
    for (parts, slots, got, _), arrivals in zip(plan, gots):
        b_held, b_sem, g_held, g_sem = (refs.pop(0) for _ in range(4))
        start = 0
        for i, (a, b, lo, hi) in enumerate(parts):
            if a >= 0:
                copies.append(
                    pltpu.make_async_copy(bs[b].at[:, lo:hi], b_held.at[:, start : start + hi - lo], b_sem.at[i])
                )
            start += hi - lo
        for i, ((at_rows, first, last, col), g) in enumerate(zip(got, arrivals)):
            for p, row in enumerate(at_rows):
                src = g.at[row * step : (row + 1) * step, first:last]
                copies.append(pltpu.make_async_copy(src, g_held.at[i, p, :, col : col + last - first], g_sem.at[i, p]))
        work.append((b_held, g_held))
    for c in copies:
        c.start()
    if mix:
        dres = ins[0][...]
        for r in ins[1:]:
            dres = dres + r[...].astype(F32)
        if dres_out is not None:
            dres_out[...] = dres
        dres_turned[...] = dres.T.astype(BF)
    for c in copies:
        c.wait()
    for h, tu in zip(held, turned):
        if tu is not None:
            turn_blocks(h, tu)
    for (parts, slots, got, targets), (b_held, g_held) in zip(plan, work):
        for p, e in enumerate(slots):
            start = 0
            for (a, _, lo, hi), (form, o, place) in zip(parts, targets):
                cols = slice(start, start + hi - lo)
                if form is not None and form != e:
                    start += hi - lo
                    continue
                if a < 0:
                    rows = dres_turned[rows_at((e % sub) ^ (d & (sub - 1)), step), :]
                    value = dot(rows, z_held[(e // sub) ^ (d // sub)])
                else:
                    value = slot_product(held[a], turned[a], e ^ by, step, b_held[:, cols])
                for i, (_, first, last, col) in enumerate(got):
                    if col <= start and start + hi - lo <= col + last - first:
                        value = value + g_held[i, p, :, cols].astype(F32)
                out = outs[o]
                if form is not None:
                    out[:, place : place + hi - lo] = value.astype(out.dtype)
                else:
                    out[p * step : (p + 1) * step, place : place + hi - lo] = value.astype(out.dtype)
                start += hi - lo


def stage(idx, a_sets, mixed, bs, streams, outs, step, width, sub):
    rows = a_sets[0][0].shape[0] if a_sets else mixed[1][0].shape[0]
    args, scratch, plan, flops = [idx], [], [], 0
    specs = [SMEM]
    for blocks in a_sets:
        args += blocks
        n = sum(b.shape[1] for b in blocks) // width
        scratch += [pltpu.VMEM((n, rows, width), BF), pltpu.SemaphoreType.DMA((n,))]
        if step % 128:
            scratch.append(pltpu.VMEM((n * width, rows), BF))
    specs += [ANY] * (len(args) - 1)
    outs = list(outs)
    mix, n_z = 0, 0
    if mixed:
        ins, zs = mixed
        mix, n_z = len(ins), len(zs)
        args += ins + zs
        specs += [VMEM] * mix + [ANY] * len(zs)
        scratch += [
            pltpu.VMEM((width, rows), BF), pltpu.VMEM((len(zs), rows, width), BF), pltpu.SemaphoreType.DMA((len(zs),))
        ]
        if mix > 1:
            outs.append(shape((rows, width), F32))
    args += bs
    for parts, slots, got, targets in streams:
        args += [g[0] for g in got]
        cols = sum(hi - lo for _, _, lo, hi in parts)
        arrivals = tuple((tuple(has.index(e) for e in slots), first, last, col) for _, has, first, last, col in got)
        plan.append((tuple(parts), tuple(slots), arrivals, tuple(targets)))
        flops += 2 * rows * len(slots) * step * cols
        scratch += [
            pltpu.VMEM((rows, cols), BF),
            pltpu.SemaphoreType.DMA((len(parts),)),
            pltpu.VMEM((max(1, len(got)), len(slots), step, cols), BF),
            pltpu.SemaphoreType.DMA((max(1, len(got)), len(slots))),
        ]
    specs += [ANY] * (len(args) - len(specs))
    body = functools.partial(stage_body, tuple(plan), mix, n_z, tuple(len(a) for a in a_sets), sub, step)
    return call(body, args, specs, outs, scratch, flops, 16)


def ffn_end_body(cut, turns, one, two, got_one, got_two, gate, up, down):
    hidden = gate.shape[1]
    gate[...] = one[:, :hidden] + got_one[:, :hidden].astype(F32)
    up[...] = two[:, :hidden] + got_two[:, :hidden].astype(F32)
    low = one[:, hidden:] + got_one[:, hidden:].astype(F32)
    if turns:
        down[:cut, :] = low.T
    else:
        down[:, :cut] = low
    if cut < hidden:
        high = two[:, hidden:] + got_two[:, hidden:].astype(F32)
        if turns:
            down[cut:, :] = high.T
        else:
            down[:, cut:] = high


def io_end_body(cut, one, two, got_one, got_two, out):
    width = out.shape[2]
    low = one[...] + got_one[...].astype(F32)
    high = two[...] + got_two[...].astype(F32)
    for k in range(3):
        at = k * width
        out[k] = low[:, at : at + width] if at < cut else high[:, at - cut : at - cut + width]


def last_body(nt, turns, *refs):
    smalls, (piece_one, piece_two, conv, mid, norm, out) = refs[:nt], refs[nt:]
    conv[...] = smalls[0][0:3, :]
    mid[...] = sum(r[4 + j : 5 + j, :] for j, r in enumerate(smalls))
    norm[...] = sum(r[4 + nt + j : 5 + nt + j, :] for j, r in enumerate(smalls))
    piece = piece_one[...].astype(F32) + piece_two[...].astype(F32)
    out[...] = piece.T if turns else piece


def per_device(nd, nt, block_in, norm_in, w_in, conv_w, w_out, norm_mid, w_gate, w_up, w_down, cot):
    t = lax.axis_index("tensor")
    d = lax.axis_index("dp")
    rows, width = block_in.shape[1:]
    feats = w_in.shape[0]
    hidden = w_gate.shape[1]
    sub = nd // nt
    step = feats // nd
    bits = list(range(nd.bit_length() - 1))
    order_one = bits
    order_two = bits[:1] + bits[2:3] + bits[1:2] + bits[3:]
    plan_one, plan_two = slot_plan(order_one), slot_plan(order_two)
    idx = jnp.stack([t, d, d ^ (sub * t)]).astype(jnp.int32)

    def over_tensor(arr, j):
        return lax.ppermute(arr, "tensor", [(i, i ^ j) for i in range(nt)])

    def over_dp(arr, e):
        return lax.ppermute(arr, "dp", [(i, i ^ e) for i in range(nd)])

    def gather(arr):
        return [over_tensor(arr, j) for j in range(1, nt)]

    def scatter(arrs):
        return [over_tensor(a, j + 1) for j, a in enumerate(arrs)]

    gains = jnp.stack([norm_in, norm_mid]).reshape(2 * nt, width)
    x_own = block_in[0]
    gy_own = cot[0]
    gain = norm_in[:width]
    for k in range(1, nt):
        gain = jnp.where(t == k, norm_in[k * width : (k + 1) * width], gain)
    x0 = (x_own * gain[None]).astype(BF)
    xs = gather(x0)
    w_three = jnp.transpose(w_in, (1, 0, 2))

    share = width // nd
    part = lax.dynamic_slice_in_dim(w_out, d * share, share, axis=0)
    shares = gather(part)
    held = [jnp.stack(shares)[None]]
    groups = [[0]]
    if nd == 8:
        for e in (2, 4, 6):
            held.append(over_dp(held[0], e))
            groups.append([e])
        for e in (0, 2, 4, 6):
            held.append(over_dp(held[e // 2], 1))
            groups.append([e + 1])
    else:
        for b in bits:
            whole = jnp.concatenate(held, axis=0)
            held.append(over_dp(whole, 1 << b))
            groups.append([e | (1 << b) for e in range(1 << b)])
    groups = tuple(tuple(g) for g in groups)

    zmix, proj, conv, q1 = call(
        functools.partial(mixer_body, nt),
        [idx, x_own, x0] + xs + [gains, w_three, conv_w],
        [SMEM] + [VMEM] * (4 + nt),
        [shape((rows, width), BF), shape((rows, 3 * width), F32), shape((rows, width), F32), shape((rows, 1), F32)],
        [],
        2 * rows * w_in.size,
        8,
    )
    zs = gather(zmix)
    c0 = gy_own.astype(BF)
    cs = [c0] + gather(c0)

    block = shape((rows, width), BF)
    blockf = shape((rows, width), F32)
    wide = shape((rows, hidden), F32)
    wideb = shape((rows, hidden), BF)
    resid, q2, h2, gpre, upre, act, wo = call(
        functools.partial(forward_body, nt, groups),
        [idx, x_own] + xs + [gains, zmix] + zs + [w_out] + held + [w_gate, w_up],
        [SMEM] + [VMEM] * (nt + 2 + nt) + [ANY] * len(held) + [VMEM] * 2,
        [shape((rows, feats), F32), shape((rows, 1), F32), shape((rows, feats), BF), wide, wide, wideb]
        + [shape((nt - 1, width, feats), BF)],
        [pltpu.SemaphoreType.DMA((nd,))],
        2 * rows * (feats * feats + 2 * feats * hidden),
        4,
    )
    dgate, dup, dz, mids, *rest = call(
        functools.partial(backward_body, nt),
        [idx] + cs + [gains, resid, q2, gpre, upre, w_out, wo, w_gate, w_up, w_down],
        [SMEM] + [VMEM] * (nt + 10),
        [wideb, wideb, blockf, shape((nt, width), F32)] + [block] * nt + [block] * (nt - 1),
        [],
        2 * rows * (2 * feats * feats + 3 * feats * hidden),
        8,
    )
    es, zgs = rest[:nt], rest[nt:]
    zgs = scatter(zgs)
    e_got = scatter(es[1:])

    def sent(msg, e, slots):
        return over_dp(msg, e), [s ^ e for s in slots]

    def run(a_sets, mixed, bs, streams, outs):
        return stage(idx, a_sets, mixed, bs, streams, outs, step, width, sub)

    cut = (hidden // 128 + 1) // 2 * 128 if hidden % 128 == 0 else hidden
    bs = [dgate, dup, act]
    one = [(0, 0, 0, hidden), (1, 2, 0, cut)]
    two = [(0, 1, 0, hidden), (1, 2, cut, hidden)]
    total_one, total_two = hidden + cut, 2 * hidden - cut
    flat_one = [(None, 0, 0), (None, 0, hidden)]
    flat_two = [(None, 1, 0), (None, 1, hidden)]
    keep_one = [(0, 2, 0), (0, 2, hidden)]
    keep_two = [(0, 3, 0), (0, 3, hidden)]
    slots = plan_one[0][0]
    (msg,) = run(
        [[h2], cs], None, bs,
        [(one + two, slots, [], flat_one + [(None, 0, total_one), (None, 0, total_one + hidden)])],
        [shape((len(slots) * step, total_one + total_two), BF)],
    )
    got = sent(msg, 1 << bits[0], slots)
    got_one = [got + (0, total_one, 0)]
    got_two = [got + (total_one, total_one + total_two, 0)]
    for i in range(1, len(bits)):
        s_one, s_two = plan_one[i][0], plan_two[i][0]
        streams = [(one, s_one, got_one, flat_one), (two, s_two, got_two, flat_two)]
        outs = [shape((len(s_one) * step, total_one), BF), shape((len(s_two) * step, total_two), BF)]
        if i == len(bits) - 1:
            streams += [(one, [0], got_one, keep_one), (two, [0], got_two, keep_two)]
            outs += [shape((step, total_one), F32), shape((step, total_two), F32)]
        m_one, m_two, *kept = run([[h2], cs], None, bs, streams, outs)
        last_one = sent(m_one, 1 << order_one[i], s_one)
        last_two = sent(m_two, 1 << order_two[i], s_two)
        got_one = got_one + [last_one + (0, total_one, 0)]
        got_two = got_two + [last_two + (0, total_two, 0)]
    turns = step % 128 == 0
    down = shape((hidden, step) if turns else (step, hidden), F32)
    s_gate, s_up, s_down = call(
        functools.partial(ffn_end_body, cut, turns),
        kept + [last_one[0], last_two[0]], [VMEM] * 4, [shape((step, hidden), F32)] * 2 + [down], [], 0, 12,
    )
    if not turns:
        s_down = s_down.T

    x_all = [x0] + xs
    slots = plan_two[0][0]
    extra = [pltpu.VMEM((feats, rows), BF)] if step % 128 else []
    message = shape((2 * rows, width), BF)
    n_vec = (4 + 2 * nt + 7) // 8 * 8
    dproj, u_own, out_own, vec, first, *us = call(
        functools.partial(mixer_back_body, nt, tuple(slots), step),
        [idx, dz] + zgs + [x_own, proj, conv, q1, gains, mids, conv_w, resid[:, :width]]
        + x_all + [w_three, w_down, act],
        [SMEM] + [VMEM] * (1 + (nt - 1) + 8) + [ANY] * nt + [VMEM] * 3,
        [shape((rows, 3 * width), BF), blockf, blockf, shape((n_vec, width), F32), shape((len(slots) * step, 3 * width), BF)]
        + [message] * (nt - 1),
        [pltpu.VMEM((nt, rows, width), BF), pltpu.SemaphoreType.DMA((nt,))] + extra,
        2 * rows * (2 * w_in.size + w_down.size),
        8,
    )
    cols = 3 * width
    split = 2 * width
    sin = sent(first, 1 << order_two[0], slots)
    small = vec
    for b in bits:
        small = small + over_dp(small, 1 << b)
    us = scatter(us)

    z_all = [zmix] + zs
    ins = [gy_own, es[0]] + e_got
    msg, dres = run(
        [], (ins, z_all), [gy_own], [([(-1, 0, 0, width)], slots, [], [(None, 0, 0)])],
        [shape((len(slots) * step, width), BF)],
    )
    smix = sent(msg, 1 << order_two[0], slots)
    high = cols - split
    got_one = [sin + (0, split, 0)]
    got_two = [sin + (split, cols, 0), smix + (0, width, high)]
    one = [(0, 0, 0, split)]
    two = [(0, 0, split, cols), (-1, 0, 0, width)]
    for i in range(1, len(bits)):
        s_one, s_two = plan_one[i][0], plan_two[i][0]
        if i < len(bits) - 1:
            m_one, m_two = run(
                [x_all], ([dres], z_all), [dproj],
                [(one, s_one, got_one, [(None, 0, 0)]), (two, s_two, got_two, [(None, 1, 0), (None, 1, high)])],
                [shape((len(s_one) * step, split), BF), shape((len(s_two) * step, high + width), BF)],
            )
        else:
            piece = shape((step, width), BF)
            m_one, m_two, kept_one, kept_two, far, near = run(
                [x_all], ([dres], z_all), [dproj],
                [
                    (one, s_one, got_one, [(None, 0, 0)]),
                    (two, s_two, got_two, [(None, 1, 0), (None, 4, 0)]),
                    (one, [0], got_one, [(0, 2, 0)]),
                    (two, [0], got_two, [(0, 3, 0), (None, 5, 0)]),
                ],
                [
                    shape((step, split), BF), shape((step, high), BF), shape((step, split), F32), shape((step, high), F32),
                    piece, piece,
                ],
            )
        end_one = sent(m_one, 1 << order_one[i], s_one)
        end_two = sent(m_two, 1 << order_two[i], s_two)
        got_one = got_one + [end_one + (0, split, 0)]
        got_two = got_two + [end_two + (0, high + width, 0)]
    s_in = call(
        functools.partial(io_end_body, split),
        [kept_one, kept_two, end_one[0], end_two[0]], [VMEM] * 4, [shape((3, step, width), F32)], [], 0, 8,
    )[0]
    s_in = jnp.transpose(s_in, (1, 0, 2))

    def home(piece, e):
        return lax.ppermute(
            piece, ("dp", "tensor"),
            [
                (a * nt + b, (sub * b + (a ^ e) % sub) * nt + (b ^ ((a ^ e) // sub)))
                for a in range(nd) for b in range(nt)
            ],
        )

    pieces = [home(far, 1 << order_two[-1]), home(near, 0)]

    dx, out = call(
        functools.partial(finish_body, nt), [dres, u_own, out_own] + us, [VMEM] * (3 + nt - 1), [blockf, blockf], [], 0, 8
    )
    smalls = [small] + gather(small)
    row = shape((1, width), F32)
    s_conv, s_mid, s_norm, s_out = call(
        functools.partial(last_body, nt, turns), smalls + pieces, [VMEM] * (nt + 2),
        [shape((3, width), F32), row, row, shape((width, step) if turns else (step, width), F32)], [], 0, 8,
    )
    if not turns:
        s_out = s_out.T
    return (
        out[None],
        dx[None],
        s_norm[0],
        s_in,
        s_conv,
        s_out,
        s_mid[0],
        s_gate,
        s_up,
        s_down,
    )


def solution(mesh):
    placed = (
        P("dp", None, "tensor"),
        P(),
        P(None, None, "tensor"),
        P(None, "tensor"),
        P("tensor", None),
        P(),
        P(None, "tensor"),
        P(None, "tensor"),
        P("tensor", None),
        P("dp", None, "tensor"),
    )

    def body(*args):
        return per_device(mesh.shape["dp"], mesh.shape["tensor"], *args)

    return jax.shard_map(
        body,
        mesh=mesh,
        in_specs=placed,
        out_specs=(
            P("dp", None, "tensor"),
            P("dp", None, "tensor"),
            P("tensor"),
            P("dp", None, "tensor"),
            P(None, "tensor"),
            P("tensor", "dp"),
            P("tensor"),
            P("dp", "tensor"),
            P("dp", "tensor"),
            P("tensor", "dp"),
        ),
        check_vma=False,
    )
```
